512 devices in a mesh: row: 32 (over x, y), col: 16 (over z, core).
Axes of the slice: x: 4, y: 8, z: 8, core: 2. Of those that a mesh axis runs over, the one named last changes fastest.
Arguments:
- rhs: bfloat16 [5, 32, 32, 256], P(None, 'row'), may hold values from -6 to 6
- factor: bfloat16 [10, 32, 32, 256, 256], P(None, 'col', 'row'), may hold values from -0.0625 to 0.0625
- pattern: int32 [10, 32, 32], P(None, 'col', 'row'), may hold values 0 or 1
- diag_inverse: bfloat16 [5, 32, 256, 256], P(None, 'row'), as said below
Outputs:
- forward: bfloat16 [5, 32, 32, 256], P(None, 'row')
- solution: bfloat16 [5, 32, 32, 256], P(None, 'row')
The draws below stay inside these ranges and needn't reach their ends.
Inputs may be any that keep to these rules, and one draw needn't show every extreme that they name: Each block of diag_inverse is lower triangular with a positive diagonal.
All inputs are finite; a program needn't handle non-finite values. No bound on the sum of `pattern` on one device may be relied on, other than what follows from the above.
Results may differ from the reference program's by a relative error of at most 0.028.
Values may be sent and summed in bfloat16 or wider, within the bound.
A program may use at most 64 MiB of HBM per device.

```python
import jax
import jax.numpy as jnp

W = 256
R = 32
LV = 5
M = 32
PAIRS = 10


def draw_diag_inverse(key, part):
    key_diag, key_low = jax.random.split(jax.random.fold_in(key, 17))
    diag = jnp.exp(jax.random.uniform(key_diag, (LV, M, W), jnp.float32, jnp.log(0.5), jnp.log(1.5)))
    low = jnp.clip(jax.random.normal(key_low, (LV, M, W, W), jnp.float32), -3.0, 3.0)
    rows = jnp.arange(W)[:, None]
    cols = jnp.arange(W)[None, :]
    strict = (rows > cols).astype(jnp.float32)
    unit = (rows == cols).astype(jnp.float32)
    values = low * (0.5 / jnp.sqrt(jnp.float32(W))) * strict + diag[:, :, :, None] * unit
    return values.astype(jnp.bfloat16)


def touch_ends(drawn, key, low, largest):
    index_at = [jax.random.randint(jax.random.fold_in(key, axis), (), 0, length) for axis, length in enumerate(drawn.shape)]
    main_axis = drawn.shape.index(max(drawn.shape))
    beside = index_at[:main_axis] + [(index_at[main_axis] + 1) % drawn.shape[main_axis]] + index_at[main_axis + 1:]
    return drawn.at[tuple(index_at)].set(low).at[tuple(beside)].set(largest)


def steps_of(stream_key, shape, cuts, smallest, largest):
    factor_of = 1.0
    for dim, shards_of in cuts:
        heights = jax.random.uniform(jax.random.fold_in(jax.random.fold_in(stream_key, 6), dim), (shards_of,), jnp.float32, smallest / len(cuts), largest / len(cuts))
        factor_of = factor_of * jnp.repeat(jnp.exp(heights), shape[dim] // shards_of).reshape((-1,) + (1,) * (len(shape) - 1 - dim))
    return factor_of


def normal_values(stream_key, dims, width, reach, cuts=(), held_as=jnp.bfloat16):
    gain = steps_of(stream_key, dims, cuts, -0.22, 0.18) if cuts else 1.0
    drawn = jax.random.normal(stream_key, dims, jnp.float32) * width * gain
    return jnp.minimum(jnp.maximum(drawn, -reach), reach).astype(held_as)


def setup_inputs(seed: int = 0) -> dict:
    keys = jax.random.split(jax.random.key(seed), 5)
    return {
        "rhs": normal_values(keys[0], (LV, M, R, W), 1.0, 6.0, ((1, 32),)),
        "factor": normal_values(keys[1], (PAIRS, M, M, W, W), (M * W * (LV - 1) // 4) ** -0.5, 0.0625, ((1, 16), (2, 32))),
        "pattern": touch_ends((jax.random.randint(keys[2], (PAIRS, M, M), 0, 4) < 3).astype(jnp.int32), jax.random.fold_in(keys[2], 1), 0, 1),
        "diag_inverse": draw_diag_inverse(jax.random.fold_in(keys[4], 71), 0),
    }


def pair_index(later, earlier):
    return later * (later - 1) // 2 + earlier


def reference(rhs, factor, pattern, diag_inverse):
    mask_f = pattern.astype(jnp.float32)
    forward_list = []
    for level in range(LV):
        if level == 0:
            zeta = rhs[0]
        else:
            total = jnp.zeros((M, R, W), jnp.float32)
            for earlier in range(level):
                index = pair_index(level, earlier)
                blocks = factor[index].astype(jnp.float32)
                prod = jnp.einsum('tsij,srj->tsri', blocks, forward_list[earlier].astype(jnp.float32))
                total = total + jnp.sum(prod * mask_f[index][:, :, None, None], axis=1)
            zeta = (rhs[level].astype(jnp.float32) - total).astype(jnp.bfloat16)
        solved = jnp.einsum('mrj,mij->mri', zeta.astype(jnp.float32), diag_inverse[level].astype(jnp.float32))
        forward_list.append(solved.astype(jnp.bfloat16))
    back_list = [None] * LV
    for level in range(LV - 1, -1, -1):
        if level == LV - 1:
            zeta = forward_list[level]
        else:
            total = jnp.zeros((M, R, W), jnp.float32)
            for later in range(LV - 1, level, -1):
                index = pair_index(later, level)
                blocks = factor[index].astype(jnp.float32)
                prod = jnp.einsum('tri,tsij->tsrj', back_list[later].astype(jnp.float32), blocks)
                total = total + jnp.sum(prod * mask_f[index][:, :, None, None], axis=0)
            zeta = (forward_list[level].astype(jnp.float32) - total).astype(jnp.bfloat16)
        solved = jnp.einsum('mri,mij->mrj', zeta.astype(jnp.float32), diag_inverse[level].astype(jnp.float32))
        back_list[level] = solved.astype(jnp.bfloat16)
    return jnp.stack(forward_list), jnp.stack(back_list)
```

```python
import functools

import jax
import jax.numpy as jnp
from jax import lax
from jax.experimental import pallas as pl
from jax.experimental.pallas import tpu as pltpu
from jax.sharding import PartitionSpec as P

MESH = pl.DeviceIdType.MESH
BF16 = jnp.bfloat16
F32 = jnp.float32


def pair_index(later, earlier):
    return later * (later - 1) // 2 + earlier


def times_transposed(left, right):
    return lax.dot_general(left, right, (((1,), (1,)), ((), ())), preferred_element_type=F32)


def times(left, right):
    return lax.dot_general(left, right, (((1,), (0,)), ((), ())), preferred_element_type=F32)


def kernel(
    levels, rows, cols,
    rhs, factor, pattern, diag, forward_out, solution_out,
    fsend, arecv, fbuf, usend, rrecv, sbuf, pbuf,
    a_send, a_recv, b_send, b_recv, r_send, r_recv, p_send, p_recv, s_send, s_recv,
):
    row = lax.axis_index("row")
    col = lax.axis_index("col")
    core = col % 2
    chip = col // 2
    home_col = row // 2
    home_chip = home_col // 2
    at_home = chip == home_chip
    own_slot = row % 2
    is_self = at_home & (col == home_col)
    half = fsend.shape[3]
    width = rhs.shape[-1]

    def remote(src, dst, send_sem, recv_sem, device):
        return pltpu.make_async_remote_copy(
            src_ref=src, dst_ref=dst, send_sem=send_sem, recv_sem=recv_sem, device_id=device, device_id_type=MESH
        )

    def send(src, dst, send_sem, recv_sem, device):
        same = (device[0] == row) & (device[1] == col)

        @pl.when(same)
        def _():
            pltpu.make_async_copy(src, dst, recv_sem).start()

        @pl.when(jnp.logical_not(same))
        def _():
            remote(src, dst, send_sem, recv_sem, device).start()

    def await_recv(ref, sem):
        remote(ref, ref, sem, sem, (row, col)).wait_recv()

    def await_send(count, sem):
        ref = arecv.at[0, pl.ds(0, count)]
        remote(ref, ref, sem, sem, (row, col)).wait_send()

    barrier = pltpu.get_barrier_semaphore()

    def greet(device):
        same = (device[0] == row) & (device[1] == col)

        @pl.when(jnp.logical_not(same))
        def _():
            pl.semaphore_signal(barrier, inc=1, device_id=device, device_id_type=MESH)

    for h in range(2):
        greet((row, home_chip * 2 + h))
        for j in range(2):
            greet((2 * col + j, chip * 2 + h))

    @pl.when(at_home)
    def _():
        def along_rows(i, _):
            greet(((row + i) % rows, home_col))
            return 0

        def along_cols(i, _):
            greet((row, (col + i) % cols))
            return 0

        lax.fori_loop(0, rows, along_rows, 0)
        lax.fori_loop(1, cols, along_cols, 0)

    def mask(index, j):
        return pattern[index, j, 0].astype(F32)

    def both(ref):
        return ref[...].reshape(2 * half, width)

    def fterm(later, earlier, j):
        index = pair_index(later, earlier)
        return times_transposed(both(fbuf.at[earlier]), factor[2 * index + j]) * mask(index, j)

    def bterm(later, earlier, j):
        index = pair_index(later, earlier)
        return times(both(pbuf.at[later, j]), factor[2 * index + j]) * mask(index, j)

    def solve_and_spread(level, zeta):
        sbuf[level, core] = times(zeta, diag[level]).astype(BF16)
        if level > 0:

            def along_rows(i, _):
                to = (row + i) % rows
                send(
                    sbuf.at[level, core], pbuf.at[level, own_slot, core],
                    p_send.at[level - 1], p_recv.at[level - 1], (to, home_col),
                )
                return 0

            lax.fori_loop(0, rows, along_rows, 0)

        def along_cols(i, _):
            to = (col + i) % cols
            remote(sbuf.at[level, core], sbuf.at[level, core], s_send.at[level], s_recv.at[level], (row, to)).start()
            return 0

        lax.fori_loop(1, cols, along_cols, 0)

    def await_halves(buf, sem):
        @pl.when(at_home)
        def _():
            await_recv(buf.at[0], sem)

        @pl.when(jnp.logical_not(at_home))
        def _():
            await_recv(buf, sem)

    first = times_transposed(rhs[0], diag[0]).astype(BF16)
    fbuf[0] = first.reshape(2, half, width)
    lower = [fterm(1, 0, j) for j in range(2)]

    for level in range(1, levels):
        at = level - 1
        for j in range(2):
            fsend[at, j] = lower[j].astype(BF16).reshape(2, half, width)
        if level == 1:

            @pl.when(jnp.logical_not(at_home))
            def _():
                pl.semaphore_wait(barrier, 6)

            @pl.when(at_home & jnp.logical_not(is_self))
            def _():
                pl.semaphore_wait(barrier, 5 + rows + cols - 1)

            @pl.when(is_self)
            def _():
                pl.semaphore_wait(barrier, 5 + rows + cols - 1 - 2)

        for j in range(2):
            for h in range(2):
                send(fsend.at[at, j, h], arecv.at[at, row], a_send.at[at], a_recv.at[at], (2 * col + j, chip * 2 + h))

        if level + 1 < levels:
            early = [sum(fterm(level + 1, b, j) for b in range(level)) for j in range(2)]

        @pl.when(at_home)
        def _():
            await_recv(arecv.at[at], a_recv.at[at])
            total = jnp.sum(arecv[at].astype(F32), axis=0)
            zeta = (rhs[level, pl.ds(pl.multiple_of(core * half, half), half)].astype(F32) - total).astype(BF16)
            fbuf[level, core] = times_transposed(zeta, diag[level]).astype(BF16)

            if level == levels - 1:
                solve_and_spread(level, fbuf[level, core])

            def along(i, _):
                to = (col + i) % cols
                remote(fbuf.at[level, core], fbuf.at[level, core], b_send.at[at], b_recv.at[at], (row, to)).start()
                return 0

            lax.fori_loop(1, cols, along, 0)

        if level + 1 < levels:
            await_halves(fbuf.at[level], b_recv.at[at])
            lower = [early[j] + fterm(level + 1, level, j) for j in range(2)]

    early = None
    for level in range(levels - 2, -1, -1):
        await_recv(pbuf.at[level + 1], p_recv.at[level])
        upper = bterm(level + 1, level, 0) + bterm(level + 1, level, 1)
        if early is not None:
            upper = upper + early
        usend[level] = upper.astype(BF16).reshape(2, half, width)
        for h in range(2):
            send(usend.at[level, h], rrecv.at[level, col], r_send.at[level], r_recv.at[level], (row, home_chip * 2 + h))
        if level > 0:
            early = sum(bterm(later, level - 1, j) for later in range(level + 1, levels) for j in range(2))

        @pl.when(at_home)
        def _():
            await_recv(rrecv.at[level], r_recv.at[level])
            total = jnp.sum(rrecv[level].astype(F32), axis=0)
            solve_and_spread(level, (fbuf[level, core].astype(F32) - total).astype(BF16))

    await_halves(fbuf.at[levels - 1], b_recv.at[levels - 2])
    forward_out[...] = fbuf[...].reshape(forward_out.shape)
    for level in range(levels - 1, -1, -1):
        await_halves(sbuf.at[level], s_recv.at[level])
        solution_out[level] = both(sbuf.at[level])

    for at in range(levels - 1):

        @pl.when(is_self)
        def _():
            await_send(3, a_send.at[at])
            await_send(1, r_send.at[at])

        @pl.when(jnp.logical_not(is_self))
        def _():
            await_send(4, a_send.at[at])

            @pl.when(at_home)
            def _():
                await_send(1, r_send.at[at])

            @pl.when(jnp.logical_not(at_home))
            def _():
                await_send(2, r_send.at[at])

        @pl.when(at_home)
        def _():
            await_send(cols - 1, b_send.at[at])

            @pl.when(is_self)
            def _():
                await_send(rows - 1, p_send.at[at])

            @pl.when(jnp.logical_not(is_self))
            def _():
                await_send(rows, p_send.at[at])

    @pl.when(at_home)
    def _():
        for level in range(levels):
            await_send(cols - 1, s_send.at[level])


def on_device(rhs, factor, pattern, diag_inverse):
    levels, _, count, width = rhs.shape
    pairs, block_rows = factor.shape[:2]
    rows, cols = lax.axis_size("row"), lax.axis_size("col")
    half = count // 2
    steps = levels - 1
    vmem = pl.BlockSpec(memory_space=pltpu.VMEM)
    dma = pltpu.SemaphoreType.DMA
    out = jax.ShapeDtypeStruct((levels, count, width), BF16)
    forward, solved = pl.pallas_call(
        functools.partial(kernel, levels, rows, cols),
        out_shape=(out, out),
        in_specs=[vmem, vmem, pl.BlockSpec(memory_space=pltpu.SMEM), vmem],
        out_specs=(vmem, vmem),
        scratch_shapes=[
            pltpu.VMEM((steps, 2, 2, half, width), BF16),
            pltpu.VMEM((steps, rows, half, width), BF16),
            pltpu.VMEM((levels, 2, half, width), BF16),
            pltpu.VMEM((steps, 2, half, width), BF16),
            pltpu.VMEM((steps, cols, half, width), BF16),
            pltpu.VMEM((levels, 2, half, width), BF16),
            pltpu.VMEM((levels, 2, 2, half, width), BF16),
        ]
        + [dma((steps,))] * 8
        + [dma((levels,))] * 2,
        compiler_params=pltpu.CompilerParams(collective_id=0, has_side_effects=True, vmem_limit_bytes=32 << 20),
        name="solves",
    )(
        rhs.reshape(levels, count, width),
        factor.reshape(pairs * block_rows, width, width),
        pattern,
        diag_inverse.reshape(levels, width, width),
    )
    return forward.reshape(rhs.shape), solved.reshape(rhs.shape)


def solution(mesh):
    return jax.shard_map(
        on_device,
        mesh=mesh,
        in_specs=(
            P(None, "row", None, None),
            P(None, "col", "row", None, None),
            P(None, "col", "row"),
            P(None, "row", None, None),
        ),
        out_specs=(P(None, "row", None, None), P(None, "row", None, None)),
        check_vma=False,
    )
```

```python
import functools

import jax
import jax.numpy as jnp
from jax import lax
from jax.experimental import pallas as pl
from jax.experimental.pallas import tpu as pltpu
from jax.sharding import PartitionSpec as P

MESH = pl.DeviceIdType.MESH
BF16 = jnp.bfloat16
F32 = jnp.float32


def pair_index(later, earlier):
    return later * (later - 1) // 2 + earlier


def times_transposed(left, right):
    return lax.dot_general(left, right, (((1,), (1,)), ((), ())), preferred_element_type=F32)


def times(left, right):
    return lax.dot_general(left, right, (((1,), (0,)), ((), ())), preferred_element_type=F32)


def kernel(
    levels, rows, cols,
    rhs_hbm, factor_hbm, pattern, diag_hbm, forward_out, solution_out,
    rhs, factor, diag, fsend, arecv, fbuf, usend, rrecv, sbuf, pbuf,
    a_send, a_recv, b_send, b_recv, r_send, r_recv, p_send, p_recv, s_send, s_recv, loaded,
):
    row = lax.axis_index("row")
    col = lax.axis_index("col")
    core = col % 2
    chip = col // 2
    home_col = row // 2
    home_chip = home_col // 2
    at_home = chip == home_chip
    own_slot = row % 2
    is_self = at_home & (col == home_col)
    half = fsend.shape[3]
    width = rhs.shape[-1]

    def remote(src, dst, send_sem, recv_sem, device):
        return pltpu.make_async_remote_copy(
            src_ref=src, dst_ref=dst, send_sem=send_sem, recv_sem=recv_sem, device_id=device, device_id_type=MESH
        )

    def send(src, dst, send_sem, recv_sem, device):
        same = (device[0] == row) & (device[1] == col)

        @pl.when(same)
        def _():
            pltpu.make_async_copy(src, dst, recv_sem).start()

        @pl.when(jnp.logical_not(same))
        def _():
            remote(src, dst, send_sem, recv_sem, device).start()

    def await_recv(ref, sem):
        remote(ref, ref, sem, sem, (row, col)).wait_recv()

    def await_send(count, sem):
        ref = arecv.at[0, pl.ds(0, count)]
        remote(ref, ref, sem, sem, (row, col)).wait_send()

    loads = [
        pltpu.make_async_copy(src, dst, loaded.at[n])
        for n, (src, dst) in enumerate(
            [
                (rhs_hbm, rhs),
                (diag_hbm.at[0], diag.at[0]),
                (factor_hbm.at[pl.ds(0, 2)], factor.at[pl.ds(0, 2)]),
                (diag_hbm.at[pl.ds(1, levels - 1)], diag.at[pl.ds(1, levels - 1)]),
                (factor_hbm.at[pl.ds(2, factor.shape[0] - 2)], factor.at[pl.ds(2, factor.shape[0] - 2)]),
            ]
        )
    ]
    for load in loads:
        load.start()

    barrier = pltpu.get_barrier_semaphore()

    def greet(device):
        same = (device[0] == row) & (device[1] == col)

        @pl.when(jnp.logical_not(same))
        def _():
            pl.semaphore_signal(barrier, inc=1, device_id=device, device_id_type=MESH)

    def around(n, size):
        return (size // 2 + (1 - 2 * (n % 2)) * ((n + 1) // 2)) % size

    def row_at(n):
        return (row // 8 + around(n % 4, 4)) % 4 * 8 + (row + around(n // 4, 8)) % 8

    def col_at(n):
        return (chip + around(n // 2, 8)) % 8 * 2 + (core + 1 - n % 2) % 2

    @pl.when(at_home)
    def _():
        def along_rows(n, _):
            greet((row_at(n), home_col))
            return 0

        lax.fori_loop(0, rows, along_rows, 0)

    for h in range(2):
        greet((row, home_chip * 2 + h))

    def mask(index, j):
        return pattern[j, 0, index].astype(F32)

    def both(ref):
        return ref[...].reshape(2 * half, width)

    def fterm(later, earlier, j):
        index = pair_index(later, earlier)
        return times_transposed(both(fbuf.at[earlier]), factor[2 * index + j]) * mask(index, j)

    def bterm(later, earlier, j):
        index = pair_index(later, earlier)
        return times(both(pbuf.at[later, j]), factor[2 * index + j]) * mask(index, j)

    def solve_and_spread(level, zeta):
        sbuf[level, core] = times(zeta, diag[level]).astype(BF16)
        half_solved, at = sbuf.at[level, core], level - 1

        def along_rows(n, _):
            to = (row_at(n), home_col)
            remote(half_solved, pbuf.at[level, own_slot, core], p_send.at[at], p_recv.at[at], to).start()
            return 0

        lax.fori_loop(0, rows - 1, along_rows, 0)
        send(half_solved, pbuf.at[level, own_slot, core], p_send.at[at], p_recv.at[at], (row, home_col))

        def along_cols(n, _):
            remote(half_solved, half_solved, s_send.at[level], s_recv.at[level], (row, col_at(n))).start()
            return 0

        lax.fori_loop(0, cols - 1, along_cols, 0)

    def await_halves(buf, sem):
        @pl.when(at_home)
        def _():
            await_recv(buf.at[0], sem)

        @pl.when(jnp.logical_not(at_home))
        def _():
            await_recv(buf, sem)

    loads[0].wait()
    loads[1].wait()
    first = times_transposed(rhs[0], diag[0]).astype(BF16)
    fbuf[0] = first.reshape(2, half, width)
    loads[2].wait()
    lower = [fterm(1, 0, j) for j in range(2)]

    for level in range(1, levels):
        at = level - 1
        for j in range(2):
            fsend[at, j] = lower[j].astype(BF16).reshape(2, half, width)
        if level == 1:

            @pl.when(jnp.logical_not(at_home))
            def _():
                pl.semaphore_wait(barrier, 4)

            @pl.when(at_home & jnp.logical_not(is_self))
            def _():
                pl.semaphore_wait(barrier, 4 + cols - 1)

            @pl.when(is_self)
            def _():
                pl.semaphore_wait(barrier, 3 + cols - 1)

        for j in range(2):
            for h in range(2):
                send(fsend.at[at, j, h], arecv.at[at, row], a_send.at[at], a_recv.at[at], (2 * col + j, chip * 2 + h))

        if level == 1:
            loads[3].wait()
            loads[4].wait()
        if level + 1 < levels:
            early = [sum(fterm(level + 1, b, j) for b in range(level)) for j in range(2)]

        @pl.when(at_home)
        def _():
            await_recv(arecv.at[at], a_recv.at[at])
            total = jnp.sum(arecv[at].astype(F32), axis=0)
            zeta = (rhs[level, pl.ds(pl.multiple_of(core * half, half), half)].astype(F32) - total).astype(BF16)
            fbuf[level, core] = times_transposed(zeta, diag[level]).astype(BF16)

            if level == levels - 1:
                solve_and_spread(level, fbuf[level, core])

            def along(n, _):
                to = (row, col_at(n))
                remote(fbuf.at[level, core], fbuf.at[level, core], b_send.at[at], b_recv.at[at], to).start()
                return 0

            lax.fori_loop(0, cols - 1, along, 0)

        if level + 1 < levels:
            await_halves(fbuf.at[level], b_recv.at[at])
            lower = [early[j] + fterm(level + 1, level, j) for j in range(2)]

    early = None
    for level in range(levels - 2, -1, -1):
        await_recv(pbuf.at[level + 1], p_recv.at[level])
        upper = bterm(level + 1, level, 0) + bterm(level + 1, level, 1)
        if early is not None:
            upper = upper + early
        usend[level] = upper.astype(BF16).reshape(2, half, width)
        if level > 0:
            for h in range(2):
                to = (row, home_chip * 2 + h)
                send(usend.at[level, h], rrecv.at[level, col], r_send.at[level], r_recv.at[level], to)
            early = sum(bterm(later, level - 1, j) for later in range(level + 1, levels) for j in range(2))

            @pl.when(at_home)
            def _():
                await_recv(rrecv.at[level], r_recv.at[level])
                total = jnp.sum(rrecv[level].astype(F32), axis=0)
                solve_and_spread(level, (fbuf[level, core].astype(F32) - total).astype(BF16))

    def to_chips(n, _):
        to_chip = (chip + around(n, 8)) % 8
        for h in range(2):
            remote(usend.at[0, h], rrecv.at[0, col], r_send.at[0], r_recv.at[0], (row, to_chip * 2 + h)).start()
        return 0

    lax.fori_loop(0, cols // 2 - 1, to_chips, 0)
    other = (row, chip * 2 + 1 - core)
    remote(usend.at[0, 1 - core], rrecv.at[0, col], r_send.at[0], r_recv.at[0], other).start()
    pltpu.make_async_copy(usend.at[0, core], rrecv.at[0, col], r_recv.at[0]).start()

    await_halves(fbuf.at[levels - 1], b_recv.at[levels - 2])
    forward_out[...] = fbuf[...].reshape(forward_out.shape)
    for level in range(levels - 1, 0, -1):
        await_halves(sbuf.at[level], s_recv.at[level])
        solution_out[level] = both(sbuf.at[level])

    await_recv(rrecv.at[0], r_recv.at[0])
    total = jnp.sum(rrecv[0].astype(F32), axis=0)
    zeta = (fbuf[0, core].astype(F32) - total).astype(BF16)
    sbuf[0, core] = times(zeta, diag[0]).astype(BF16)
    remote(sbuf.at[0, core], sbuf.at[0, core], s_send.at[0], s_recv.at[0], other).start()
    await_recv(sbuf.at[0, 0], s_recv.at[0])
    solution_out[0] = both(sbuf.at[0])

    await_send(1, s_send.at[0])
    await_send(cols - 1, r_send.at[0])
    for at in range(levels - 1):

        @pl.when(is_self)
        def _():
            await_send(3, a_send.at[at])

        @pl.when(jnp.logical_not(is_self))
        def _():
            await_send(4, a_send.at[at])

        if at > 0:

            @pl.when(at_home)
            def _():
                await_send(1, r_send.at[at])

            @pl.when(jnp.logical_not(at_home))
            def _():
                await_send(2, r_send.at[at])

        @pl.when(at_home)
        def _():
            await_send(cols - 1, b_send.at[at])

            @pl.when(is_self)
            def _():
                await_send(rows - 1, p_send.at[at])

            @pl.when(jnp.logical_not(is_self))
            def _():
                await_send(rows, p_send.at[at])

    @pl.when(at_home)
    def _():
        for level in range(1, levels):
            await_send(cols - 1, s_send.at[level])


def on_device(rhs, factor, pattern, diag_inverse):
    levels, _, count, width = rhs.shape
    pairs, block_rows = factor.shape[:2]
    rows, cols = lax.axis_size("row"), lax.axis_size("col")
    half = count // 2
    steps = levels - 1
    vmem, hbm = pl.BlockSpec(memory_space=pltpu.VMEM), pl.BlockSpec(memory_space=pltpu.HBM)
    dma = pltpu.SemaphoreType.DMA
    out = jax.ShapeDtypeStruct((levels, count, width), BF16)
    forward, solved = pl.pallas_call(
        functools.partial(kernel, levels, rows, cols),
        out_shape=(out, out),
        in_specs=[hbm, hbm, pl.BlockSpec(memory_space=pltpu.SMEM), hbm],
        out_specs=(vmem, vmem),
        scratch_shapes=[
            pltpu.VMEM((levels, count, width), BF16),
            pltpu.VMEM((pairs * block_rows, width, width), BF16),
            pltpu.VMEM((levels, width, width), BF16),
            pltpu.VMEM((steps, 2, 2, half, width), BF16),
            pltpu.VMEM((steps, rows, half, width), BF16),
            pltpu.VMEM((levels, 2, half, width), BF16),
            pltpu.VMEM((steps, 2, half, width), BF16),
            pltpu.VMEM((steps, cols, half, width), BF16),
            pltpu.VMEM((levels, 2, half, width), BF16),
            pltpu.VMEM((levels, 2, 2, half, width), BF16),
        ]
        + [dma((steps,))] * 8
        + [dma((levels,))] * 3,
        compiler_params=pltpu.CompilerParams(collective_id=0, has_side_effects=True),
        name="solves",
    )(
        rhs.reshape(levels, count, width),
        factor.reshape(pairs * block_rows, width, width),
        pattern.transpose(1, 2, 0),
        diag_inverse.reshape(levels, width, width),
    )
    return forward.reshape(rhs.shape), solved.reshape(rhs.shape)


def solution(mesh):
    return jax.shard_map(
        on_device,
        mesh=mesh,
        in_specs=(
            P(None, "row", None, None),
            P(None, "col", "row", None, None),
            P(None, "col", "row"),
            P(None, "row", None, None),
        ),
        out_specs=(P(None, "row", None, None), P(None, "row", None, None)),
        check_vma=False,
    )
```

```python
import functools

import jax
import jax.numpy as jnp
from jax import lax
from jax.experimental import pallas as pl
from jax.experimental.pallas import tpu as pltpu
from jax.sharding import PartitionSpec as P

MESH = pl.DeviceIdType.MESH
BF16 = jnp.bfloat16
F32 = jnp.float32


def pair_index(later, earlier):
    return later * (later - 1) // 2 + earlier


def times_transposed(left, right):
    return lax.dot_general(left, right, (((1,), (1,)), ((), ())), preferred_element_type=F32)


def times(left, right):
    return lax.dot_general(left, right, (((1,), (0,)), ((), ())), preferred_element_type=F32)


def kernel(
    levels, rows, cols,
    rhs_hbm, factor_hbm, pattern, diag_hbm, forward_out, solution_out,
    rhs, factor, diag, fsend, arecv, zbuf, ebuf, usend, rrecv, sq, sbuf, pbuf, usend0, rrecv0, sbuf0, stop, ptop,
    a_send, a_recv, b_send, b_recv, r_send, r_recv, p_send, p_recv, s_send, s_recv, loaded,
):
    row = lax.axis_index("row")
    col = lax.axis_index("col")
    core = col % 2
    chip = col // 2
    home_col = row // 2
    home_chip = home_col // 2
    at_home = chip == home_chip
    own_slot = row % 2
    is_self = at_home & (col == home_col)
    is_server = ((row // 4) % 2 == chip % 2) & ((row // 2) % 2 == core)
    served_row = chip // 2 * 8 + row % 8
    quarter = row // 8
    top = levels - 1
    half = fsend.shape[3]
    width = rhs.shape[-1]

    def remote(src, dst, send_sem, recv_sem, device):
        return pltpu.make_async_remote_copy(
            src_ref=src, dst_ref=dst, send_sem=send_sem, recv_sem=recv_sem, device_id=device, device_id_type=MESH
        )

    def send(src, dst, send_sem, recv_sem, device):
        same = (device[0] == row) & (device[1] == col)

        @pl.when(same)
        def _():
            pltpu.make_async_copy(src, dst, recv_sem).start()

        @pl.when(jnp.logical_not(same))
        def _():
            remote(src, dst, send_sem, recv_sem, device).start()

    def await_recv(ref, sem):
        remote(ref, ref, sem, sem, (row, col)).wait_recv()

    def await_sends(count, sem, slots):
        ref = slots.at[0, pl.ds(0, count)]
        remote(ref, ref, sem, sem, (row, col)).wait_send()

    pairs = [(later, earlier) for later in range(1, levels) for earlier in range(later)]
    loads = [
        pltpu.make_async_copy(src, dst, loaded.at[n])
        for n, (src, dst) in enumerate(
            [
                (rhs_hbm, rhs),
                (diag_hbm.at[0], diag.at[0]),
                (factor_hbm.at[pl.ds(0, 2)], factor.at[pl.ds(0, 2)]),
                (diag_hbm.at[pl.ds(1, levels - 1)], diag.at[pl.ds(1, levels - 1)]),
                (factor_hbm.at[pl.ds(2, factor.shape[0] - 2)], factor.at[pl.ds(2, factor.shape[0] - 2)]),
            ]
        )
    ]
    for load in loads:
        load.start()

    barrier = pltpu.get_barrier_semaphore()

    def greet(device):
        same = (device[0] == row) & (device[1] == col)

        @pl.when(jnp.logical_not(same))
        def _():
            pl.semaphore_signal(barrier, inc=1, device_id=device, device_id_type=MESH)

    def around(n, size):
        return (size // 2 + (1 - 2 * (n % 2)) * ((n + 1) // 2)) % size

    def row_at(n):
        return (row // 8 + around(n % 4, 4)) % 4 * 8 + (row + around(n // 4, 8)) % 8

    def col_at(n):
        return (chip + around(n // 2, 8)) % 8 * 2 + (core + 1 - n % 2) % 2

    def repeat(count, step):
        def body(n, _):
            step(n)
            return 0

        lax.fori_loop(0, count, body, 0)

    @pl.when(at_home)
    def _():
        repeat(rows, lambda n: greet((row_at(n), home_col)))

    for h in range(2):
        greet((row, home_chip * 2 + h))

    def fold(later, earlier):
        index = pair_index(later, earlier)

        def one(j):
            block = times(factor[2 * index + j], diag[earlier]) * pattern[j, 0, index].astype(F32)
            factor[2 * index + j] = block.astype(BF16)

        repeat(2, one)

    def joined(ref):
        return ref[...].reshape(2 * half, width)

    def zeta_of(level):
        return rhs[0] if level == 0 else joined(zbuf.at[level])

    def fterm(later, earlier, j):
        return times_transposed(zeta_of(earlier), factor[2 * pair_index(later, earlier) + j])

    def bterm(later, earlier, j):
        solved = joined(ptop.at[j] if later == top else pbuf.at[later, j])
        return times(solved, factor[2 * pair_index(later, earlier) + j])

    def finish_forward(level):
        solved = times_transposed(zeta_of(level), diag[level]).astype(BF16)
        forward_out[level] = solved
        ebuf[level] = times(solved, diag[level])

    def await_halves(buf, sem):
        @pl.when(at_home)
        def _():
            await_recv(buf.at[0], sem)

        @pl.when(jnp.logical_not(at_home))
        def _():
            await_recv(buf, sem)

    def to_column(src, dst, send_sem, recv_sem):
        repeat(cols - 1, lambda n: remote(src, dst, send_sem, recv_sem, (row, col_at(n))).start())

    for load in loads[:3]:
        load.wait()
    fold(1, 0)
    lower = [fterm(1, 0, j) for j in range(2)]

    for level in range(1, levels):
        at = level - 1
        for j in range(2):
            fsend[at, j] = lower[j].astype(BF16).reshape(2, half, width)
        if level == 1:

            @pl.when(jnp.logical_not(at_home))
            def _():
                pl.semaphore_wait(barrier, 4)

            @pl.when(at_home & jnp.logical_not(is_self))
            def _():
                pl.semaphore_wait(barrier, 4 + cols - 1)

            @pl.when(is_self)
            def _():
                pl.semaphore_wait(barrier, 3 + cols - 1)

        for j in range(2):
            for h in range(2):
                send(fsend.at[at, j, h], arecv.at[at, row], a_send.at[at], a_recv.at[at], (2 * col + j, chip * 2 + h))

        if level == 1:
            loads[3].wait()
            loads[4].wait()
            for later, earlier in pairs[1:]:
                fold(later, earlier)
        if level + 1 < levels:
            early = [sum(fterm(level + 1, b, j) for b in range(level)) for j in range(2)]
        finish_forward(level - 1)

        @pl.when(at_home)
        def _():
            await_recv(arecv.at[at], a_recv.at[at])
            total = jnp.sum(arecv[at].astype(F32), axis=0)
            zeta = (rhs[level, pl.ds(pl.multiple_of(core * half, half), half)].astype(F32) - total).astype(BF16)
            if level < top:
                zbuf[level, core] = zeta
            else:
                solved = times_transposed(zeta, diag[top]).astype(BF16)
                zbuf[top, core] = solved
                stop[core] = times(solved, diag[top]).astype(BF16)
                slot = ptop.at[own_slot, core]
                repeat(
                    rows - 1,
                    lambda n: remote(
                        stop.at[core], slot, p_send.at[top - 1], p_recv.at[top - 1], (row_at(n), home_col)
                    ).start(),
                )
                send(stop.at[core], slot, p_send.at[top - 1], p_recv.at[top - 1], (row, home_col))
                to_column(stop.at[core], stop.at[core], s_send.at[top], s_recv.at[top])
            to_column(zbuf.at[level, core], zbuf.at[level, core], b_send.at[at], b_recv.at[at])

        if level < top:
            await_halves(zbuf.at[level], b_recv.at[at])
            lower = [early[j] + fterm(level + 1, level, j) for j in range(2)]

    early = None
    for level in range(top - 1, -1, -1):
        await_recv(ptop if level + 1 == top else pbuf.at[level + 1], p_recv.at[level])
        upper = bterm(level + 1, level, 0) + bterm(level + 1, level, 1)
        if early is not None:
            upper = upper + early
        if level > 0:
            mine = jnp.where(col == home_col, ebuf[level] - upper, -upper)
            usend[level] = mine.astype(BF16).reshape(usend.shape[1:])
            for q in range(4):
                to = (q * 8 + row % 8, home_col)
                send(usend.at[level, q], rrecv.at[level, col], r_send.at[level], r_recv.at[level], to)
            early = sum(bterm(later, level - 1, j) for later in range(level + 1, levels) for j in range(2))

            @pl.when(is_server)
            def _():
                slots = rrecv.at[level, pl.ds(0, cols)]
                await_recv(slots, r_recv.at[level])
                sq[level] = jnp.sum(slots[...].astype(F32), axis=0).astype(BF16)
                at = level - 1

                def spread(n):
                    to = (row_at(n), col)
                    remote(sq.at[level], pbuf.at[level, own_slot, quarter], p_send.at[at], p_recv.at[at], to).start()

                repeat(rows - 1, spread)
                pltpu.make_async_copy(sq.at[level], pbuf.at[level, own_slot, quarter], p_recv.at[at]).start()

                def give(n):
                    to = (served_row, col_at(n))
                    remote(sq.at[level], sbuf.at[level, quarter], s_send.at[level], s_recv.at[level], to).start()

                repeat(cols - 1, give)
                to = (served_row, col)
                send(sq.at[level], sbuf.at[level, quarter], s_send.at[level], s_recv.at[level], to)

    usend0[...] = upper.astype(BF16).reshape(usend0.shape)

    def to_chips(n):
        to_chip = (chip + around(n, 8)) % 8
        for h in range(2):
            remote(usend0.at[h], rrecv0.at[0, col], r_send.at[0], r_recv.at[0], (row, to_chip * 2 + h)).start()

    repeat(cols // 2 - 1, to_chips)
    other = (row, chip * 2 + 1 - core)
    remote(usend0.at[1 - core], rrecv0.at[0, col], r_send.at[0], r_recv.at[0], other).start()
    pltpu.make_async_copy(usend0.at[core], rrecv0.at[0, col], r_recv.at[0]).start()

    await_halves(zbuf.at[top], b_recv.at[top - 1])
    forward_out[top] = joined(zbuf.at[top])
    await_halves(stop, s_recv.at[top])
    solution_out[top] = joined(stop)
    for level in range(top - 1, 0, -1):
        await_recv(sbuf.at[level], s_recv.at[level])
        solution_out[level] = joined(sbuf.at[level])

    await_recv(rrecv0.at[0], r_recv.at[0])
    total = jnp.sum(rrecv0[0].astype(F32), axis=0)
    mine = ebuf[0, pl.ds(pl.multiple_of(core * half, half), half)]
    sbuf0[core] = (mine - total).astype(BF16)
    remote(sbuf0.at[core], sbuf0.at[core], s_send.at[0], s_recv.at[0], other).start()
    await_recv(sbuf0.at[0], s_recv.at[0])
    solution_out[0] = joined(sbuf0)

    await_sends(1, s_send.at[0], rrecv0)
    await_sends(cols - 1, r_send.at[0], rrecv0)
    for at in range(top):

        @pl.when(is_self)
        def _():
            await_sends(3, a_send.at[at], arecv)

        @pl.when(jnp.logical_not(is_self))
        def _():
            await_sends(4, a_send.at[at], arecv)

        @pl.when(at_home)
        def _():
            await_sends(cols - 1, b_send.at[at], arecv)

    @pl.when(at_home)
    def _():
        await_sends(cols - 1, s_send.at[top], arecv)

        @pl.when(is_self)
        def _():
            await_sends(rows - 1, p_send.at[top - 1], arecv)

        @pl.when(jnp.logical_not(is_self))
        def _():
            await_sends(rows, p_send.at[top - 1], arecv)

    for level in range(1, top):

        @pl.when(is_self)
        def _():
            await_sends(3, r_send.at[level], rrecv)
            await_sends(cols - 1, s_send.at[level], rrecv)

        @pl.when(jnp.logical_not(is_self))
        def _():
            await_sends(4, r_send.at[level], rrecv)

        @pl.when(is_server)
        def _():
            await_sends(rows - 1, p_send.at[level - 1], rrecv)

        @pl.when(is_server & jnp.logical_not(is_self))
        def _():
            await_sends(cols, s_send.at[level], rrecv)


def on_device(rhs, factor, pattern, diag_inverse):
    levels, _, count, width = rhs.shape
    pairs, block_rows = factor.shape[:2]
    rows, cols = lax.axis_size("row"), lax.axis_size("col")
    half = count // 2
    steps = levels - 1
    vmem, hbm = pl.BlockSpec(memory_space=pltpu.VMEM), pl.BlockSpec(memory_space=pltpu.HBM)
    dma = pltpu.SemaphoreType.DMA
    out = pltpu.VMEM((levels, count, width), BF16)
    forward, solved = pl.pallas_call(
        functools.partial(kernel, levels, rows, cols),
        out_shape=(out, out),
        in_specs=[hbm, hbm, pl.BlockSpec(memory_space=pltpu.SMEM), hbm],
        out_specs=(vmem, vmem),
        scratch_shapes=[
            pltpu.VMEM((levels, count, width), BF16),
            pltpu.VMEM((pairs * block_rows, width, width), BF16),
            pltpu.VMEM((levels, width, width), BF16),
            pltpu.VMEM((steps, 2, 2, half, width), BF16),
            pltpu.VMEM((steps, rows, half, width), BF16),
            pltpu.VMEM((levels, 2, half, width), BF16),
            pltpu.VMEM((steps, count, width), F32),
            pltpu.VMEM((steps, 4, half // 2, width), BF16),
            pltpu.VMEM((steps, rows, half // 2, width), BF16),
            pltpu.VMEM((steps, half // 2, width), BF16),
            pltpu.VMEM((steps, 4, half // 2, width), BF16),
            pltpu.VMEM((steps, 2, 4, half // 2, width), BF16),
            pltpu.VMEM((2, half, width), BF16),
            pltpu.VMEM((1, cols, half, width), BF16),
            pltpu.VMEM((2, half, width), BF16),
            pltpu.VMEM((2, half, width), BF16),
            pltpu.VMEM((2, 2, half, width), BF16),
        ]
        + [dma((steps,))] * 8
        + [dma((levels,))] * 3,
        compiler_params=pltpu.CompilerParams(collective_id=0, has_side_effects=True),
        name="solves",
    )(
        rhs.reshape(levels, count, width),
        factor.reshape(pairs * block_rows, width, width),
        pattern.transpose(1, 2, 0),
        diag_inverse.reshape(levels, width, width),
    )
    return forward.reshape(rhs.shape), solved.reshape(rhs.shape)


def solution(mesh):
    return jax.shard_map(
        on_device,
        mesh=mesh,
        in_specs=(
            P(None, "row", None, None),
            P(None, "col", "row", None, None),
            P(None, "col", "row"),
            P(None, "row", None, None),
        ),
        out_specs=(P(None, "row", None, None), P(None, "row", None, None)),
        check_vma=False,
    )
```

```python
import functools

import jax
import jax.numpy as jnp
from jax import lax
from jax.experimental import pallas as pl
from jax.experimental.pallas import tpu as pltpu
from jax.sharding import PartitionSpec as P

MESH = pl.DeviceIdType.MESH
BF16 = jnp.bfloat16
F32 = jnp.float32


def pair_index(later, earlier):
    return later * (later - 1) // 2 + earlier


def times_transposed(left, right):
    return lax.dot_general(left, right, (((1,), (1,)), ((), ())), preferred_element_type=F32)


def times(left, right):
    return lax.dot_general(left, right, (((1,), (0,)), ((), ())), preferred_element_type=F32)


def kernel(
    levels, rows, cols,
    rhs_hbm, factor_hbm, pattern, diag_hbm, forward_out, solution_out,
    rhs, factor, diag, dtop, fsend, arecv, zbuf, ebuf, ftop_send, atop, fq, ftop, usend, rrecv, sq, sbuf, pbuf,
    usend0, rrecv0, sbuf0,
    a_send, a_recv, b_send, b_recv, r_send, r_recv, p_send, p_recv, s_send, s_recv, loaded, d_send, d_recv,
):
    row = lax.axis_index("row")
    col = lax.axis_index("col")
    core = col % 2
    chip = col // 2
    home_col = row // 2
    home_chip = home_col // 2
    at_home = chip == home_chip
    own_slot = row % 2
    is_self = at_home & (col == home_col)
    is_server = ((row // 4) % 2 == chip % 2) & ((row // 2) % 2 == core)
    served_row = chip // 2 * 8 + row % 8
    quarter = row // 8
    top = levels - 1
    half = fsend.shape[3]
    width = rhs.shape[-1]

    def remote(src, dst, send_sem, recv_sem, device):
        return pltpu.make_async_remote_copy(
            src_ref=src, dst_ref=dst, send_sem=send_sem, recv_sem=recv_sem, device_id=device, device_id_type=MESH
        )

    def send(src, dst, send_sem, recv_sem, device):
        same = (device[0] == row) & (device[1] == col)

        @pl.when(same)
        def _():
            pltpu.make_async_copy(src, dst, recv_sem).start()

        @pl.when(jnp.logical_not(same))
        def _():
            remote(src, dst, send_sem, recv_sem, device).start()

    def await_recv(ref, sem):
        remote(ref, ref, sem, sem, (row, col)).wait_recv()

    def await_sends(count, sem, slots):
        ref = slots.at[0, pl.ds(0, count)]
        remote(ref, ref, sem, sem, (row, col)).wait_send()

    pairs = [(later, earlier) for later in range(1, levels) for earlier in range(later)]
    loads = [
        pltpu.make_async_copy(src, dst, loaded.at[n])
        for n, (src, dst) in enumerate(
            [
                (rhs_hbm, rhs),
                (diag_hbm.at[0], diag.at[0]),
                (factor_hbm.at[pl.ds(0, 2)], factor.at[pl.ds(0, 2)]),
                (diag_hbm.at[pl.ds(1, levels - 1)], diag.at[pl.ds(1, levels - 1)]),
                (factor_hbm.at[pl.ds(2, factor.shape[0] - 2)], factor.at[pl.ds(2, factor.shape[0] - 2)]),
            ]
        )
    ]
    for load in loads:
        load.start()

    barrier = pltpu.get_barrier_semaphore()

    def greet(device):
        same = (device[0] == row) & (device[1] == col)

        @pl.when(jnp.logical_not(same))
        def _():
            pl.semaphore_signal(barrier, inc=1, device_id=device, device_id_type=MESH)

    def around(n, size):
        return (size // 2 + (1 - 2 * (n % 2)) * ((n + 1) // 2)) % size

    def row_at(n):
        return (row // 8 + around(n % 4, 4)) % 4 * 8 + (row + around(n // 4, 8)) % 8

    def col_at(n):
        return (chip + around(n // 2, 8)) % 8 * 2 + (core + 1 - n % 2) % 2

    def repeat(count, step):
        def body(n, _):
            step(n)
            return 0

        lax.fori_loop(0, count, body, 0)

    @pl.when(at_home)
    def _():
        repeat(rows, lambda n: greet((row_at(n), home_col)))

    for h in range(2):
        greet((row, home_chip * 2 + h))

    def fold(later, earlier):
        index = pair_index(later, earlier)

        def one(j):
            block = times(factor[2 * index + j], diag[earlier]) * pattern[j, 0, index].astype(F32)
            factor[2 * index + j] = block.astype(BF16)

        repeat(2, one)

    def joined(ref):
        return ref[...].reshape(2 * half, width)

    def zeta_of(level):
        return rhs[0] if level == 0 else joined(zbuf.at[level])

    def fterm(later, earlier, j):
        return times_transposed(zeta_of(earlier), factor[2 * pair_index(later, earlier) + j])

    def bterm(later, earlier, j):
        return times(joined(pbuf.at[later, j]), factor[2 * pair_index(later, earlier) + j])

    def finish_forward(level):
        solved = times_transposed(zeta_of(level), diag[level]).astype(BF16)
        forward_out[level] = solved
        ebuf[level] = times(solved, diag[level])

    def await_halves(buf, sem):
        @pl.when(at_home)
        def _():
            await_recv(buf.at[0], sem)

        @pl.when(jnp.logical_not(at_home))
        def _():
            await_recv(buf, sem)

    def serve(level):
        at = level - 1

        def spread(n):
            to = (row_at(n), col)
            remote(sq.at[level], pbuf.at[level, own_slot, quarter], p_send.at[at], p_recv.at[at], to).start()

        repeat(rows - 1, spread)
        pltpu.make_async_copy(sq.at[level], pbuf.at[level, own_slot, quarter], p_recv.at[at]).start()
        give(sq.at[level], sbuf.at[level, quarter], s_send.at[level], s_recv.at[level])

    def give(src, dst, send_sem, recv_sem):
        repeat(cols - 1, lambda n: remote(src, dst, send_sem, recv_sem, (served_row, col_at(n))).start())
        send(src, dst, send_sem, recv_sem, (served_row, col))

    for load in loads[:3]:
        load.wait()
    fold(1, 0)
    lower = [fterm(1, 0, j) for j in range(2)]

    for level in range(1, top):
        at = level - 1
        for j in range(2):
            fsend[at, j] = lower[j].astype(BF16).reshape(2, half, width)
        if level == 1:

            @pl.when(jnp.logical_not(at_home))
            def _():
                pl.semaphore_wait(barrier, 4)

            @pl.when(at_home & jnp.logical_not(is_self))
            def _():
                pl.semaphore_wait(barrier, 4 + cols - 1)

            @pl.when(is_self)
            def _():
                pl.semaphore_wait(barrier, 3 + cols - 1)

        for j in range(2):
            for h in range(2):
                send(fsend.at[at, j, h], arecv.at[at, row], a_send.at[at], a_recv.at[at], (2 * col + j, chip * 2 + h))

        if level == 1:
            loads[3].wait()
            loads[4].wait()
            for later, earlier in pairs[1:]:
                fold(later, earlier)
        early = [sum(fterm(level + 1, b, j) for b in range(level)) for j in range(2)]
        finish_forward(level - 1)

        @pl.when(at_home)
        def _():
            await_recv(arecv.at[at], a_recv.at[at])
            total = jnp.sum(arecv[at].astype(F32), axis=0)
            own_half = rhs[level, pl.ds(pl.multiple_of(core * half, half), half)].astype(F32)
            zbuf[level, core] = (own_half - total).astype(BF16)
            own = zbuf.at[level, core]
            repeat(cols - 1, lambda n: remote(own, own, b_send.at[at], b_recv.at[at], (row, col_at(n))).start())

        await_halves(zbuf.at[level], b_recv.at[at])
        lower = [early[j] + fterm(level + 1, level, j) for j in range(2)]
        if level == 1:

            @pl.when(is_self)
            def _():
                for q in range(4):
                    send(diag.at[top], dtop, d_send, d_recv, (q * 8 + row % 8, home_col))

    at = top - 1
    for j in range(2):
        mine = jnp.where(is_self & (own_slot == j), rhs[top].astype(F32) - lower[j], -lower[j])
        ftop_send[j] = mine.astype(BF16).reshape(ftop_send.shape[1:])
    for j in range(2):
        for q in range(4):
            to = (q * 8 + (2 * col + j) % 8, col)
            send(ftop_send.at[j, q], atop.at[row], a_send.at[at], a_recv.at[at], to)
    finish_forward(top - 1)

    @pl.when(is_server)
    def _():
        await_recv(dtop, d_recv)
        await_recv(atop, a_recv.at[at])
        zeta = jnp.sum(atop[...].astype(F32), axis=0).astype(BF16)
        fq[...] = times_transposed(zeta, dtop[...]).astype(BF16)
        sq[top] = times(fq[...], dtop[...]).astype(BF16)
        serve(top)
        give(fq, ftop.at[quarter], b_send.at[at], b_recv.at[at])

    early = None
    for level in range(top - 1, -1, -1):
        await_recv(pbuf.at[level + 1], p_recv.at[level])
        upper = bterm(level + 1, level, 0) + bterm(level + 1, level, 1)
        if early is not None:
            upper = upper + early
        if level > 0:
            mine = jnp.where(col == home_col, ebuf[level] - upper, -upper)
            usend[level] = mine.astype(BF16).reshape(usend.shape[1:])
            for q in range(4):
                to = (q * 8 + row % 8, home_col)
                send(usend.at[level, q], rrecv.at[level, col], r_send.at[level], r_recv.at[level], to)
            early = sum(bterm(later, level - 1, j) for later in range(level + 1, levels) for j in range(2))

            @pl.when(is_server)
            def _():
                slots = rrecv.at[level, pl.ds(0, cols)]
                await_recv(slots, r_recv.at[level])
                sq[level] = jnp.sum(slots[...].astype(F32), axis=0).astype(BF16)
                serve(level)

    usend0[...] = upper.astype(BF16).reshape(usend0.shape)

    def to_chips(n):
        to_chip = (chip + around(n, 8)) % 8
        for h in range(2):
            remote(usend0.at[h], rrecv0.at[0, col], r_send.at[0], r_recv.at[0], (row, to_chip * 2 + h)).start()

    repeat(cols // 2 - 1, to_chips)
    other = (row, chip * 2 + 1 - core)
    remote(usend0.at[1 - core], rrecv0.at[0, col], r_send.at[0], r_recv.at[0], other).start()
    pltpu.make_async_copy(usend0.at[core], rrecv0.at[0, col], r_recv.at[0]).start()

    await_recv(ftop, b_recv.at[top - 1])
    forward_out[top] = joined(ftop)
    for level in range(top, 0, -1):
        await_recv(sbuf.at[level], s_recv.at[level])
        solution_out[level] = joined(sbuf.at[level])

    await_recv(rrecv0.at[0], r_recv.at[0])
    total = jnp.sum(rrecv0[0].astype(F32), axis=0)
    mine = ebuf[0, pl.ds(pl.multiple_of(core * half, half), half)]
    sbuf0[core] = (mine - total).astype(BF16)
    remote(sbuf0.at[core], sbuf0.at[core], s_send.at[0], s_recv.at[0], other).start()
    await_recv(sbuf0.at[0], s_recv.at[0])
    solution_out[0] = joined(sbuf0)

    await_sends(1, s_send.at[0], rrecv0)
    await_sends(cols - 1, r_send.at[0], rrecv0)
    def await_all_but(one_less, count, sem, slots):
        pl.when(one_less)(lambda: await_sends(count - 1, sem, slots))
        pl.when(jnp.logical_not(one_less))(lambda: await_sends(count, sem, slots))

    for at in range(top - 1):
        await_all_but(is_self, 4, a_send.at[at], arecv)
    await_all_but(is_server, 8, a_send.at[top - 1], rrecv)
    for level in range(1, top):
        await_all_but(is_self, 4, r_send.at[level], rrecv)

    @pl.when(at_home)
    def _():
        for at in range(top - 1):
            await_sends(cols - 1, b_send.at[at], arecv)

    @pl.when(is_server)
    def _():
        await_all_but(is_self, cols, b_send.at[top - 1], rrecv)
        for level in range(1, levels):
            await_all_but(is_self, cols, s_send.at[level], rrecv)
            await_sends(rows - 1, p_send.at[level - 1], rrecv)

    @pl.when(is_self)
    def _():
        three = factor.at[pl.ds(0, 3)]
        remote(three, three, d_send, d_send, (row, col)).wait_send()


def copy_out(forward, solved, forward_out, solution_out, sems):
    copies = [
        pltpu.make_async_copy(forward, forward_out, sems.at[0]),
        pltpu.make_async_copy(solved, solution_out, sems.at[1]),
    ]
    for copy in copies:
        copy.start()
    for copy in copies:
        copy.wait()


def on_device(rhs, factor, pattern, diag_inverse):
    levels, _, count, width = rhs.shape
    pairs, block_rows = factor.shape[:2]
    rows, cols = lax.axis_size("row"), lax.axis_size("col")
    half = count // 2
    steps = levels - 1
    vmem, hbm = pl.BlockSpec(memory_space=pltpu.VMEM), pl.BlockSpec(memory_space=pltpu.HBM)
    dma = pltpu.SemaphoreType.DMA
    out = pltpu.VMEM((levels, count, width), BF16)
    forward, solved = pl.pallas_call(
        functools.partial(kernel, levels, rows, cols),
        out_shape=(out, out),
        in_specs=[hbm, hbm, pl.BlockSpec(memory_space=pltpu.SMEM), hbm],
        out_specs=(vmem, vmem),
        scratch_shapes=[
            pltpu.VMEM((levels, count, width), BF16),
            pltpu.VMEM((pairs * block_rows, width, width), BF16),
            pltpu.VMEM((levels, width, width), BF16),
            pltpu.VMEM((width, width), BF16),
            pltpu.VMEM((steps - 1, 2, 2, half, width), BF16),
            pltpu.VMEM((steps - 1, rows, half, width), BF16),
            pltpu.VMEM((steps, 2, half, width), BF16),
            pltpu.VMEM((steps, count, width), F32),
            pltpu.VMEM((2, 4, half // 2, width), BF16),
            pltpu.VMEM((rows, half // 2, width), BF16),
            pltpu.VMEM((half // 2, width), BF16),
            pltpu.VMEM((4, half // 2, width), BF16),
            pltpu.VMEM((steps, 4, half // 2, width), BF16),
            pltpu.VMEM((steps, rows, half // 2, width), BF16),
            pltpu.VMEM((levels, half // 2, width), BF16),
            pltpu.VMEM((levels, 4, half // 2, width), BF16),
            pltpu.VMEM((levels, 2, 4, half // 2, width), BF16),
            pltpu.VMEM((2, half, width), BF16),
            pltpu.VMEM((1, cols, half, width), BF16),
            pltpu.VMEM((2, half, width), BF16),
        ]
        + [dma((steps,))] * 8
        + [dma((levels,))] * 3
        + [dma] * 2,
        compiler_params=pltpu.CompilerParams(collective_id=0, has_side_effects=True),
        name="solves",
    )(
        rhs.reshape(levels, count, width),
        factor.reshape(pairs * block_rows, width, width),
        pattern.transpose(1, 2, 0),
        diag_inverse.reshape(levels, width, width),
    )
    out = jax.ShapeDtypeStruct((levels, count, width), BF16)
    forward, solved = pl.pallas_call(
        copy_out,
        out_shape=(out, out),
        in_specs=[vmem, vmem],
        out_specs=(hbm, hbm),
        scratch_shapes=[dma((2,))],
        compiler_params=pltpu.CompilerParams(vmem_limit_bytes=1 << 20),
        name="results",
    )(forward, solved)
    return forward.reshape(rhs.shape), solved.reshape(rhs.shape)


def solution(mesh):
    return jax.shard_map(
        on_device,
        mesh=mesh,
        in_specs=(
            P(None, "row", None, None),
            P(None, "col", "row", None, None),
            P(None, "col", "row"),
            P(None, "row", None, None),
        ),
        out_specs=(P(None, "row", None, None), P(None, "row", None, None)),
        check_vma=False,
    )
```

```python
import functools

import jax
import jax.numpy as jnp
from jax import lax
from jax.experimental import pallas as pl
from jax.experimental.pallas import tpu as pltpu
from jax.sharding import PartitionSpec as P

MESH = pl.DeviceIdType.MESH
BF16 = jnp.bfloat16
F32 = jnp.float32


def pair_index(later, earlier):
    return later * (later - 1) // 2 + earlier


def times_transposed(left, right):
    return lax.dot_general(left, right, (((1,), (1,)), ((), ())), preferred_element_type=F32)


def times(left, right):
    return lax.dot_general(left, right, (((1,), (0,)), ((), ())), preferred_element_type=F32)


def kernel(
    levels, rows, cols,
    rhs_hbm, factor_hbm, pattern_hbm, diag_hbm, forward_out, solution_out,
    rhs, factor, pattern, diag, dtop, fsend, arecv, zbuf, ebuf, ftop_send, atop, fq, ftop, usend, rrecv, sq, sbuf, pbuf,
    usend0, rrecv0, sbuf0,
    a_send, a_recv, b_send, b_recv, r_send, r_recv, p_send, p_recv, s_send, s_recv, loaded, d_send, d_recv,
):
    row = lax.axis_index("row")
    col = lax.axis_index("col")
    core = col % 2
    chip = col // 2
    home_col = row // 2
    home_chip = home_col // 2
    at_home = chip == home_chip
    own_slot = row % 2
    is_self = at_home & (col == home_col)
    is_server = ((row // 4) % 2 == chip % 2) & ((row // 2) % 2 == core)
    served_row = chip // 2 * 8 + row % 8
    quarter = row // 8
    top = levels - 1
    half = fsend.shape[3]
    width = rhs.shape[-1]

    def remote(src, dst, send_sem, recv_sem, device):
        return pltpu.make_async_remote_copy(
            src_ref=src, dst_ref=dst, send_sem=send_sem, recv_sem=recv_sem, device_id=device, device_id_type=MESH
        )

    def send(src, dst, send_sem, recv_sem, device):
        same = (device[0] == row) & (device[1] == col)

        @pl.when(same)
        def _():
            pltpu.make_async_copy(src, dst, recv_sem).start()

        @pl.when(jnp.logical_not(same))
        def _():
            remote(src, dst, send_sem, recv_sem, device).start()

    def await_recv(ref, sem):
        remote(ref, ref, sem, sem, (row, col)).wait_recv()

    def await_sends(count, sem, slots):
        ref = slots.at[0, pl.ds(0, count)]
        remote(ref, ref, sem, sem, (row, col)).wait_send()

    pairs = [(later, earlier) for later in range(1, levels) for earlier in range(later)]
    loads = [
        pltpu.make_async_copy(src, dst, loaded.at[n])
        for n, (src, dst) in enumerate(
            [
                (rhs_hbm, rhs),
                (pattern_hbm, pattern),
                (diag_hbm.at[0], diag.at[0]),
                (factor_hbm.at[pl.ds(0, 2)], factor.at[pl.ds(0, 2)]),
                (diag_hbm.at[pl.ds(1, levels - 1)], diag.at[pl.ds(1, levels - 1)]),
                (factor_hbm.at[pl.ds(2, factor.shape[0] - 2)], factor.at[pl.ds(2, factor.shape[0] - 2)]),
            ]
        )
    ]
    for load in loads:
        load.start()

    barrier = pltpu.get_barrier_semaphore()

    def greet(device):
        same = (device[0] == row) & (device[1] == col)

        @pl.when(jnp.logical_not(same))
        def _():
            pl.semaphore_signal(barrier, inc=1, device_id=device, device_id_type=MESH)

    def ring(step, size):
        return min(step, size - step)

    def nearest_last(steps):
        return sorted(steps, key=lambda s: -ring(s[0], 4) - ring(s[1], 8) - ring(s[2], 8) - s[3] / 2)

    row_steps = nearest_last([(x, y, 0, 0) for x in range(4) for y in range(8)])
    col_steps = nearest_last([(0, 0, z, k) for z in range(cols // 2) for k in range(2)])
    row_by_x = [(quarter + x) % 4 * 8 for x in range(4)]
    row_by_y = [(row + y) % 8 for y in range(8)]
    col_by_z = [(chip + z) % (cols // 2) * 2 for z in range(cols // 2)]
    col_by_core = [core, 1 - core]
    plane = [row_by_x[x] + row_by_y[y] for x, y, _, _ in row_steps]
    column = [col_by_z[z] + col_by_core[k] for _, _, z, k in col_steps]

    first_rows = sorted(range(rows), key=lambda r: ring(r // 8, 4) + ring(r % 8, 8))
    chips = cols // 2

    def repeat(count, step):
        def body(n, _):
            step(n)
            return 0

        lax.fori_loop(0, count, body, 0)

    @pl.when(at_home)
    def _():
        for to_row in plane[:-1]:
            pl.semaphore_signal(barrier, inc=1, device_id=(to_row, home_col), device_id_type=MESH)
        greet((row, home_col))

    for h in range(2):
        greet((row, home_chip * 2 + h))

    def fold(later, earlier):
        index = pair_index(later, earlier)

        def one(j):
            block = times(factor[2 * index + j], diag[earlier]) * pattern[j, 0, index].astype(F32)
            factor[2 * index + j] = block.astype(BF16)

        repeat(2, one)

    def joined(ref):
        return ref[...].reshape(2 * half, width)

    def zeta_of(level):
        return rhs[0] if level == 0 else joined(zbuf.at[level])

    def fterm(later, earlier, j):
        return times_transposed(zeta_of(earlier), factor[2 * pair_index(later, earlier) + j])

    def bterm(later, earlier, j):
        return times(joined(pbuf.at[later, j]), factor[2 * pair_index(later, earlier) + j])

    def finish_forward(level):
        solved = times_transposed(zeta_of(level), diag[level]).astype(BF16)
        forward_out[level] = solved
        ebuf[level] = times(solved, diag[level])

    def await_halves(buf, sem):
        @pl.when(at_home)
        def _():
            await_recv(buf.at[0], sem)

        @pl.when(jnp.logical_not(at_home))
        def _():
            await_recv(buf, sem)

    def serve(level):
        at = level - 1
        solved, slot = sq.at[level], pbuf.at[level, own_slot, quarter]
        if level > 1:
            for to_row in plane[:-1]:
                remote(solved, slot, p_send.at[at], p_recv.at[at], (to_row, col)).start()
            pltpu.make_async_copy(solved, slot, p_recv.at[at]).start()
        else:
            for to_row in first_rows:
                send(solved, slot, p_send.at[at], p_recv.at[at], (to_row, col))
        give(solved, sbuf.at[level, quarter], s_send.at[level], s_recv.at[level])

    def give(src, dst, send_sem, recv_sem):
        for to_col in column[:-1]:
            remote(src, dst, send_sem, recv_sem, (served_row, to_col)).start()
        send(src, dst, send_sem, recv_sem, (served_row, col))

    for load in loads[:4]:
        load.wait()
    fold(1, 0)
    lower = [fterm(1, 0, j) for j in range(2)]

    for level in range(1, top):
        at = level - 1
        for j in range(2):
            fsend[at, j] = lower[j].astype(BF16).reshape(2, half, width)
        if level == 1:

            @pl.when(jnp.logical_not(at_home))
            def _():
                pl.semaphore_wait(barrier, 4)

            @pl.when(at_home & jnp.logical_not(is_self))
            def _():
                pl.semaphore_wait(barrier, 4 + cols - 1)

            @pl.when(is_self)
            def _():
                pl.semaphore_wait(barrier, 3 + cols - 1)

        for j in range(2):
            for h in range(2):
                send(fsend.at[at, j, h], arecv.at[at, row], a_send.at[at], a_recv.at[at], (2 * col + j, chip * 2 + h))

        if level == 1:
            loads[4].wait()
            loads[5].wait()
            for later, earlier in pairs[1:]:
                fold(later, earlier)
        early = [sum(fterm(level + 1, b, j) for b in range(level)) for j in range(2)]
        finish_forward(level - 1)

        @pl.when(at_home)
        def _():
            await_recv(arecv.at[at], a_recv.at[at])
            total = jnp.sum(arecv[at].astype(F32), axis=0)
            own_half = rhs[level, pl.ds(pl.multiple_of(core * half, half), half)].astype(F32)
            zbuf[level, core] = (own_half - total).astype(BF16)
            own = zbuf.at[level, core]
            for to_col in column[:-1]:
                remote(own, own, b_send.at[at], b_recv.at[at], (row, to_col)).start()

        await_halves(zbuf.at[level], b_recv.at[at])
        lower = [early[j] + fterm(level + 1, level, j) for j in range(2)]
        if level == 1:

            @pl.when(is_self)
            def _():
                for q in range(4):
                    send(diag.at[top], dtop, d_send, d_recv, (q * 8 + row % 8, home_col))

    at = top - 1
    for j in range(2):
        mine = jnp.where(is_self & (own_slot == j), rhs[top].astype(F32) - lower[j], -lower[j])
        ftop_send[j] = mine.astype(BF16).reshape(ftop_send.shape[1:])
    for j in range(2):
        for q in range(4):
            to = (q * 8 + (2 * col + j) % 8, col)
            send(ftop_send.at[j, q], atop.at[row], a_send.at[at], a_recv.at[at], to)
    finish_forward(top - 1)

    @pl.when(is_server)
    def _():
        await_recv(dtop, d_recv)
        await_recv(atop, a_recv.at[at])
        zeta = jnp.sum(atop[...].astype(F32), axis=0).astype(BF16)
        fq[...] = times_transposed(zeta, dtop[...]).astype(BF16)
        sq[top] = times(fq[...], dtop[...]).astype(BF16)
        serve(top)
        give(fq, ftop.at[quarter], b_send.at[at], b_recv.at[at])

    early = None
    for level in range(top - 1, -1, -1):
        await_recv(pbuf.at[level + 1], p_recv.at[level])
        upper = bterm(level + 1, level, 0) + bterm(level + 1, level, 1)
        if early is not None:
            upper = upper + early
        if level > 0:
            mine = jnp.where(col == home_col, ebuf[level] - upper, -upper)
            usend[level] = mine.astype(BF16).reshape(usend.shape[1:])
            for q in range(4):
                to = (q * 8 + row % 8, home_col)
                send(usend.at[level, q], rrecv.at[level, col], r_send.at[level], r_recv.at[level], to)
            early = sum(bterm(later, level - 1, j) for later in range(level + 1, levels) for j in range(2))

            @pl.when(is_server)
            def _():
                slots = rrecv.at[level, pl.ds(0, cols)]
                await_recv(slots, r_recv.at[level])
                sq[level] = jnp.sum(slots[...].astype(F32), axis=0).astype(BF16)
                serve(level)

    usend0[...] = upper.astype(BF16).reshape(usend0.shape)
    for z in range(chips):
        for k in range(2):
            for h in range(2) if z < 1 else [k]:
                send(usend0.at[h], rrecv0.at[h, col], r_send.at[0], r_recv.at[0], (row, z * 2 + k))
    starts_first = chip < 1

    await_recv(ftop, b_recv.at[top - 1])
    forward_out[top] = joined(ftop)
    for level in range(top, 0, -1):
        await_recv(sbuf.at[level], s_recv.at[level])
        solution_out[level] = joined(sbuf.at[level])

    @pl.when(starts_first)
    def _():
        await_recv(rrecv0, r_recv.at[0])
        total = jnp.sum(rrecv0[...].astype(F32), axis=1).reshape(2 * half, width)
        solution_out[0] = (ebuf[0] - total).astype(BF16)
        await_sends(cols + 2 - 2, r_send.at[0], arecv)

    @pl.when(jnp.logical_not(starts_first))
    def _():
        await_recv(rrecv0.at[core], r_recv.at[0])
        total = jnp.sum(rrecv0[core].astype(F32), axis=0)
        mine = ebuf[0, pl.ds(pl.multiple_of(core * half, half), half)]
        sbuf0[core] = (mine - total).astype(BF16)
        other = (row, chip * 2 + 1 - core)
        remote(sbuf0.at[core], sbuf0.at[core], s_send.at[0], s_recv.at[0], other).start()
        await_recv(sbuf0.at[0], s_recv.at[0])
        solution_out[0] = joined(sbuf0)
        await_sends(1, s_send.at[0], arecv)
        await_sends(cols + 2 - 1, r_send.at[0], arecv)

    def await_all_but(one_less, count, sem, slots):
        pl.when(one_less)(lambda: await_sends(count - 1, sem, slots))
        pl.when(jnp.logical_not(one_less))(lambda: await_sends(count, sem, slots))

    for at in range(top - 1):
        await_all_but(is_self, 4, a_send.at[at], arecv)
    await_all_but(is_server, 8, a_send.at[top - 1], rrecv)
    for level in range(1, top):
        await_all_but(is_self, 4, r_send.at[level], rrecv)

    @pl.when(at_home)
    def _():
        for at in range(top - 1):
            await_sends(cols - 1, b_send.at[at], arecv)

    @pl.when(is_server)
    def _():
        await_all_but(is_self, cols, b_send.at[top - 1], rrecv)
        for level in range(1, levels):
            await_all_but(is_self, cols, s_send.at[level], rrecv)
            await_sends(rows - 1, p_send.at[level - 1], rrecv)

    @pl.when(is_self)
    def _():
        three = factor.at[pl.ds(0, 3)]
        remote(three, three, d_send, d_send, (row, col)).wait_send()


def copy_out(forward, solved, forward_out, solution_out, sems):
    copies = [
        pltpu.make_async_copy(forward, forward_out, sems.at[0]),
        pltpu.make_async_copy(solved, solution_out, sems.at[1]),
    ]
    for copy in copies:
        copy.start()
    for copy in copies:
        copy.wait()


def on_device(rhs, factor, pattern, diag_inverse):
    levels, _, count, width = rhs.shape
    pairs, block_rows = factor.shape[:2]
    rows, cols = lax.axis_size("row"), lax.axis_size("col")
    half = count // 2
    steps = levels - 1
    vmem, hbm = pl.BlockSpec(memory_space=pltpu.VMEM), pl.BlockSpec(memory_space=pltpu.HBM)
    dma = pltpu.SemaphoreType.DMA
    out = pltpu.VMEM((levels, count, width), BF16)
    forward, solved = pl.pallas_call(
        functools.partial(kernel, levels, rows, cols),
        out_shape=(out, out),
        in_specs=[hbm, hbm, hbm, hbm],
        out_specs=(vmem, vmem),
        scratch_shapes=[
            pltpu.VMEM((levels, count, width), BF16),
            pltpu.VMEM((pairs * block_rows, width, width), BF16),
            pltpu.SMEM((block_rows, 1, pairs), jnp.int32),
            pltpu.VMEM((levels, width, width), BF16),
            pltpu.VMEM((width, width), BF16),
            pltpu.VMEM((steps - 1, 2, 2, half, width), BF16),
            pltpu.VMEM((steps - 1, rows, half, width), BF16),
            pltpu.VMEM((steps, 2, half, width), BF16),
            pltpu.VMEM((steps, count, width), F32),
            pltpu.VMEM((2, 4, half // 2, width), BF16),
            pltpu.VMEM((rows, half // 2, width), BF16),
            pltpu.VMEM((half // 2, width), BF16),
            pltpu.VMEM((4, half // 2, width), BF16),
            pltpu.VMEM((steps, 4, half // 2, width), BF16),
            pltpu.VMEM((steps, rows, half // 2, width), BF16),
            pltpu.VMEM((levels, half // 2, width), BF16),
            pltpu.VMEM((levels, 4, half // 2, width), BF16),
            pltpu.VMEM((levels, 2, 4, half // 2, width), BF16),
            pltpu.VMEM((2, half, width), BF16),
            pltpu.VMEM((2, cols, half, width), BF16),
            pltpu.VMEM((2, half, width), BF16),
        ]
        + [dma((steps,))] * 8
        + [dma((levels,))] * 2
        + [dma((6,))]
        + [dma] * 2,
        compiler_params=pltpu.CompilerParams(collective_id=0, has_side_effects=True),
        name="solves",
    )(
        rhs.reshape(levels, count, width),
        factor.reshape(pairs * block_rows, width, width),
        pattern.transpose(1, 2, 0),
        diag_inverse.reshape(levels, width, width),
    )
    out = jax.ShapeDtypeStruct((levels, count, width), BF16)
    forward, solved = pl.pallas_call(
        copy_out,
        out_shape=(out, out),
        in_specs=[vmem, vmem],
        out_specs=(hbm, hbm),
        scratch_shapes=[dma((2,))],
        compiler_params=pltpu.CompilerParams(vmem_limit_bytes=1 << 20),
        name="results",
    )(forward, solved)
    return forward.reshape(rhs.shape), solved.reshape(rhs.shape)


def solution(mesh):
    return jax.shard_map(
        on_device,
        mesh=mesh,
        in_specs=(
            P(None, "row", None, None),
            P(None, "col", "row", None, None),
            P(None, "col", "row"),
            P(None, "row", None, None),
        ),
        out_specs=(P(None, "row", None, None), P(None, "row", None, None)),
        check_vma=False,
    )
```

```python
import functools

import jax
import jax.numpy as jnp
from jax import lax
from jax.experimental import pallas as pl
from jax.experimental.pallas import tpu as pltpu
from jax.sharding import PartitionSpec as P

MESH = pl.DeviceIdType.MESH
BF16 = jnp.bfloat16
F32 = jnp.float32


def pair_index(later, earlier):
    return later * (later - 1) // 2 + earlier


def times_transposed(left, right):
    return lax.dot_general(left, right, (((1,), (1,)), ((), ())), preferred_element_type=F32)


def times(left, right):
    return lax.dot_general(left, right, (((1,), (0,)), ((), ())), preferred_element_type=F32)


def kernel(
    levels, rows, cols,
    rhs_hbm, factor_hbm, pattern_hbm, diag_hbm, forward_out, solution_out,
    rhs, factor, pattern, diag, dtop, fsend, arecv, zbuf, ebuf, ftop_send, atop, fq, ftop, usend, rrecv, sq, sbuf, pbuf,
    usend0, rrecv0, sbuf0,
    a_send, a_recv, b_send, b_recv, r_send, r_recv, p_send, p_recv, s_send, s_recv, loaded, d_send, d_recv, ready,
):
    row = lax.axis_index("row")
    col = lax.axis_index("col")
    core = col % 2
    chip = col // 2
    home_col = row // 2
    home_chip = home_col // 2
    at_home = chip == home_chip
    own_slot = row % 2
    is_self = at_home & (col == home_col)
    is_server = ((row // 4) % 2 == chip % 2) & ((row // 2) % 2 == core)
    served_row = chip // 2 * 8 + row % 8
    quarter = row // 8
    last = cols // 2 - 1

    def first_of(place):
        return place * (1 - place // last)

    first_chip = first_of(home_chip)
    at_first = chip == first_chip
    is_first_self = at_first & (col == home_col)
    top = levels - 1
    half = fsend.shape[3]
    width = rhs.shape[-1]

    def remote(src, dst, send_sem, recv_sem, device):
        return pltpu.make_async_remote_copy(
            src_ref=src, dst_ref=dst, send_sem=send_sem, recv_sem=recv_sem, device_id=device, device_id_type=MESH
        )

    def send(src, dst, send_sem, recv_sem, device):
        same = (device[0] == row) & (device[1] == col)

        @pl.when(same)
        def _():
            pltpu.make_async_copy(src, dst, recv_sem).start()

        @pl.when(jnp.logical_not(same))
        def _():
            remote(src, dst, send_sem, recv_sem, device).start()

    def await_recv(ref, sem):
        remote(ref, ref, sem, sem, (row, col)).wait_recv()

    def await_sends(count, sem, slots):
        ref = slots.at[0, pl.ds(0, count)]
        remote(ref, ref, sem, sem, (row, col)).wait_send()

    pairs = [(later, earlier) for later in range(1, levels) for earlier in range(later)]
    loads = [
        pltpu.make_async_copy(src, dst, loaded.at[n])
        for n, (src, dst) in enumerate(
            [
                (rhs_hbm, rhs),
                (pattern_hbm, pattern),
                (diag_hbm.at[0], diag.at[0]),
                (factor_hbm.at[pl.ds(0, 2)], factor.at[pl.ds(0, 2)]),
                (diag_hbm.at[pl.ds(1, levels - 1)], diag.at[pl.ds(1, levels - 1)]),
                (factor_hbm.at[pl.ds(2, factor.shape[0] - 2)], factor.at[pl.ds(2, factor.shape[0] - 2)]),
            ]
        )
    ]
    for load in loads:
        load.start()

    barrier = pltpu.get_barrier_semaphore()

    def greet(device):
        same = (device[0] == row) & (device[1] == col)

        @pl.when(jnp.logical_not(same))
        def _():
            pl.semaphore_signal(barrier, inc=1, device_id=device, device_id_type=MESH)

    def ring(step, size):
        return min(step, size - step)

    def nearest_last(steps):
        return sorted(steps, key=lambda s: -ring(s[0], 4) - ring(s[1], 8) - ring(s[2], 8) - s[3] / 2)

    row_steps = nearest_last([(x, y, 0, 0) for x in range(4) for y in range(8)])
    col_steps = nearest_last([(0, 0, z, k) for z in range(cols // 2) for k in range(2)])
    row_by_x = [(quarter + x) % 4 * 8 for x in range(4)]
    row_by_y = [(row + y) % 8 for y in range(8)]
    col_by_z = [(chip + z) % (cols // 2) * 2 for z in range(cols // 2)]
    col_by_core = [core, 1 - core]
    plane = [row_by_x[x] + row_by_y[y] for x, y, _, _ in row_steps]
    column = [col_by_z[z] + col_by_core[k] for _, _, z, k in col_steps]

    first_rows = sorted(range(rows), key=lambda r: ring(r // 8, 4) + ring(r % 8, 8))
    chips = cols // 2

    def repeat(count, step):
        def body(n, _):
            step(n)
            return 0

        lax.fori_loop(0, count, body, 0)

    @pl.when(at_first)
    def _():
        for to_row in plane[:-1]:
            pl.semaphore_signal(barrier, inc=1, device_id=(to_row, home_col), device_id_type=MESH)
        greet((row, home_col))

    for h in range(2):
        greet((row, first_chip * 2 + h))

    def fold(later, earlier):
        index = pair_index(later, earlier)

        def one(j):
            block = times(factor[2 * index + j], diag[earlier]) * pattern[j, 0, index].astype(F32)
            factor[2 * index + j] = block.astype(BF16)

        repeat(2, one)

    def joined(ref):
        return ref[...].reshape(2 * half, width)

    def zeta_of(level):
        return rhs[0] if level == 0 else joined(zbuf.at[level])

    def fterm(later, earlier, j):
        return times_transposed(zeta_of(earlier), factor[2 * pair_index(later, earlier) + j])

    def bterm(later, earlier, j):
        return times(joined(pbuf.at[later, j]), factor[2 * pair_index(later, earlier) + j])

    def finish_forward(level):
        solved = times_transposed(zeta_of(level), diag[level]).astype(BF16)
        forward_out[level] = solved
        ebuf[level] = times(solved, diag[level])

    def await_halves(buf, sem, has_one):
        @pl.when(has_one)
        def _():
            await_recv(buf.at[0], sem)

        @pl.when(jnp.logical_not(has_one))
        def _():
            await_recv(buf, sem)

    def serve(level):
        at = level - 1
        solved, slot = sq.at[level], pbuf.at[level, own_slot, quarter]
        if level > 1:
            for to_row in plane[:-1]:
                remote(solved, slot, p_send.at[at], p_recv.at[at], (to_row, col)).start()
            pltpu.make_async_copy(solved, slot, p_recv.at[at]).start()
        else:
            for to_row in first_rows:
                send(solved, slot, p_send.at[at], p_recv.at[at], (to_row, col))
        give(solved, sbuf.at[level, quarter], s_send.at[level], s_recv.at[level])

    def give(src, dst, send_sem, recv_sem):
        for to_col in column[:-1]:
            remote(src, dst, send_sem, recv_sem, (served_row, to_col)).start()
        send(src, dst, send_sem, recv_sem, (served_row, col))

    for load in loads[:4]:
        load.wait()
    fold(1, 0)
    lower = [fterm(1, 0, j) for j in range(2)]

    for level in range(1, top):
        at = level - 1
        for j in range(2):
            fsend[at, j] = lower[j].astype(BF16).reshape(2, half, width)
        if level == 1:

            @pl.when(jnp.logical_not(at_first))
            def _():
                pl.semaphore_wait(barrier, 4)

            @pl.when(at_first & jnp.logical_not(is_first_self))
            def _():
                pl.semaphore_wait(barrier, 4 + cols - 1)

            @pl.when(is_first_self)
            def _():
                pl.semaphore_wait(barrier, 3 + cols - 1)

        if level == 2:

            @pl.when(chip == last)
            def _():
                pl.semaphore_wait(ready, 4)

        to_chip = first_of(chip) if level == 1 else chip
        for j in range(2):
            for h in range(2):
                to = (2 * col + j, to_chip * 2 + h)
                send(fsend.at[at, j, h], arecv.at[at, row], a_send.at[at], a_recv.at[at], to)

        if level == 1:
            loads[4].wait()
            loads[5].wait()
            for later, earlier in pairs[1:]:
                fold(later, earlier)
        early = [sum(fterm(level + 1, b, j) for b in range(level)) for j in range(2)]
        finish_forward(level - 1)

        @pl.when(at_first if level == 1 else at_home)
        def _():
            await_recv(arecv.at[at], a_recv.at[at])
            total = jnp.sum(arecv[at].astype(F32), axis=0)
            own_half = rhs[level, pl.ds(pl.multiple_of(core * half, half), half)].astype(F32)
            zbuf[level, core] = (own_half - total).astype(BF16)
            own = zbuf.at[level, core]
            for to_col in column[:-1]:
                remote(own, own, b_send.at[at], b_recv.at[at], (row, to_col)).start()
            if level == 1:

                @pl.when(home_chip == last)
                def _():
                    for to_row in plane:
                        pl.semaphore_signal(ready, inc=1, device_id=(to_row, home_col), device_id_type=MESH)

        await_halves(zbuf.at[level], b_recv.at[at], at_first if level == 1 else at_home)
        lower = [early[j] + fterm(level + 1, level, j) for j in range(2)]
        if level == 1:

            @pl.when(is_self)
            def _():
                for q in range(4):
                    send(diag.at[top], dtop, d_send, d_recv, (q * 8 + row % 8, home_col))

    at = top - 1
    for j in range(2):
        mine = jnp.where(is_self & (own_slot == j), rhs[top].astype(F32) - lower[j], -lower[j])
        ftop_send[j] = mine.astype(BF16).reshape(ftop_send.shape[1:])
    for j in range(2):
        for q in range(4):
            to = (q * 8 + (2 * col + j) % 8, col)
            send(ftop_send.at[j, q], atop.at[row], a_send.at[at], a_recv.at[at], to)
    finish_forward(top - 1)

    @pl.when(is_server)
    def _():
        await_recv(dtop, d_recv)
        await_recv(atop, a_recv.at[at])
        zeta = jnp.sum(atop[...].astype(F32), axis=0).astype(BF16)
        fq[...] = times_transposed(zeta, dtop[...]).astype(BF16)
        sq[top] = times(fq[...], dtop[...]).astype(BF16)
        serve(top)
        give(fq, ftop.at[quarter], b_send.at[at], b_recv.at[at])

    early = None
    for level in range(top - 1, -1, -1):
        await_recv(pbuf.at[level + 1], p_recv.at[level])
        upper = bterm(level + 1, level, 0) + bterm(level + 1, level, 1)
        if early is not None:
            upper = upper + early
        if level > 0:
            mine = jnp.where(col == home_col, ebuf[level] - upper, -upper)
            usend[level] = mine.astype(BF16).reshape(usend.shape[1:])
            for q in range(4):
                to = (q * 8 + row % 8, home_col)
                send(usend.at[level, q], rrecv.at[level, col], r_send.at[level], r_recv.at[level], to)
            early = sum(bterm(later, level - 1, j) for later in range(level + 1, levels) for j in range(2))

            @pl.when(is_server)
            def _():
                slots = rrecv.at[level, pl.ds(0, cols)]
                await_recv(slots, r_recv.at[level])
                sq[level] = jnp.sum(slots[...].astype(F32), axis=0).astype(BF16)
                serve(level)

    usend0[...] = upper.astype(BF16).reshape(usend0.shape)
    for z in range(chips):
        for k in range(2):
            for h in range(2) if z < 1 else [k]:
                send(usend0.at[h], rrecv0.at[h, col], r_send.at[0], r_recv.at[0], (row, z * 2 + k))
    starts_first = chip < 1

    await_recv(ftop, b_recv.at[top - 1])
    forward_out[top] = joined(ftop)
    for level in range(top, 0, -1):
        await_recv(sbuf.at[level], s_recv.at[level])
        solution_out[level] = joined(sbuf.at[level])

    @pl.when(starts_first)
    def _():
        await_recv(rrecv0, r_recv.at[0])
        total = jnp.sum(rrecv0[...].astype(F32), axis=1).reshape(2 * half, width)
        solution_out[0] = (ebuf[0] - total).astype(BF16)
        await_sends(cols + 2 - 2, r_send.at[0], arecv)

    @pl.when(jnp.logical_not(starts_first))
    def _():
        await_recv(rrecv0.at[core], r_recv.at[0])
        total = jnp.sum(rrecv0[core].astype(F32), axis=0)
        mine = ebuf[0, pl.ds(pl.multiple_of(core * half, half), half)]
        sbuf0[core] = (mine - total).astype(BF16)
        other = (row, chip * 2 + 1 - core)
        remote(sbuf0.at[core], sbuf0.at[core], s_send.at[0], s_recv.at[0], other).start()
        await_recv(sbuf0.at[0], s_recv.at[0])
        solution_out[0] = joined(sbuf0)
        await_sends(1, s_send.at[0], arecv)
        await_sends(cols + 2 - 1, r_send.at[0], arecv)

    def await_all_but(one_less, count, sem, slots):
        pl.when(one_less)(lambda: await_sends(count - 1, sem, slots))
        pl.when(jnp.logical_not(one_less))(lambda: await_sends(count, sem, slots))

    for at in range(top - 1):
        await_all_but(is_first_self if at == 0 else is_self, 4, a_send.at[at], arecv)
    await_all_but(is_server, 8, a_send.at[top - 1], rrecv)
    for level in range(1, top):
        await_all_but(is_self, 4, r_send.at[level], rrecv)

    for at in range(top - 1):
        pl.when(at_first if at == 0 else at_home)(lambda at=at: await_sends(cols - 1, b_send.at[at], arecv))

    @pl.when(is_server)
    def _():
        await_all_but(is_self, cols, b_send.at[top - 1], rrecv)
        for level in range(1, levels):
            await_all_but(is_self, cols, s_send.at[level], rrecv)
            await_sends(rows - 1, p_send.at[level - 1], rrecv)

    @pl.when(is_self)
    def _():
        three = factor.at[pl.ds(0, 3)]
        remote(three, three, d_send, d_send, (row, col)).wait_send()


def copy_out(forward, solved, forward_out, solution_out, sems):
    copies = [
        pltpu.make_async_copy(forward, forward_out, sems.at[0]),
        pltpu.make_async_copy(solved, solution_out, sems.at[1]),
    ]
    for copy in copies:
        copy.start()
    for copy in copies:
        copy.wait()


def on_device(rhs, factor, pattern, diag_inverse):
    levels, _, count, width = rhs.shape
    pairs, block_rows = factor.shape[:2]
    rows, cols = lax.axis_size("row"), lax.axis_size("col")
    half = count // 2
    steps = levels - 1
    vmem, hbm = pl.BlockSpec(memory_space=pltpu.VMEM), pl.BlockSpec(memory_space=pltpu.HBM)
    dma = pltpu.SemaphoreType.DMA
    out = pltpu.VMEM((levels, count, width), BF16)
    forward, solved = pl.pallas_call(
        functools.partial(kernel, levels, rows, cols),
        out_shape=(out, out),
        in_specs=[hbm, hbm, hbm, hbm],
        out_specs=(vmem, vmem),
        scratch_shapes=[
            pltpu.VMEM((levels, count, width), BF16),
            pltpu.VMEM((pairs * block_rows, width, width), BF16),
            pltpu.SMEM((block_rows, 1, pairs), jnp.int32),
            pltpu.VMEM((levels, width, width), BF16),
            pltpu.VMEM((width, width), BF16),
            pltpu.VMEM((steps - 1, 2, 2, half, width), BF16),
            pltpu.VMEM((steps - 1, rows, half, width), BF16),
            pltpu.VMEM((steps, 2, half, width), BF16),
            pltpu.VMEM((steps, count, width), F32),
            pltpu.VMEM((2, 4, half // 2, width), BF16),
            pltpu.VMEM((rows, half // 2, width), BF16),
            pltpu.VMEM((half // 2, width), BF16),
            pltpu.VMEM((4, half // 2, width), BF16),
            pltpu.VMEM((steps, 4, half // 2, width), BF16),
            pltpu.VMEM((steps, rows, half // 2, width), BF16),
            pltpu.VMEM((levels, half // 2, width), BF16),
            pltpu.VMEM((levels, 4, half // 2, width), BF16),
            pltpu.VMEM((levels, 2, 4, half // 2, width), BF16),
            pltpu.VMEM((2, half, width), BF16),
            pltpu.VMEM((2, cols, half, width), BF16),
            pltpu.VMEM((2, half, width), BF16),
        ]
        + [dma((steps,))] * 8
        + [dma((levels,))] * 2
        + [dma((6,))]
        + [dma, dma, pltpu.SemaphoreType.REGULAR],
        compiler_params=pltpu.CompilerParams(collective_id=0, has_side_effects=True),
        name="solves",
    )(
        rhs.reshape(levels, count, width),
        factor.reshape(pairs * block_rows, width, width),
        pattern.transpose(1, 2, 0),
        diag_inverse.reshape(levels, width, width),
    )
    out = jax.ShapeDtypeStruct((levels, count, width), BF16)
    forward, solved = pl.pallas_call(
        copy_out,
        out_shape=(out, out),
        in_specs=[vmem, vmem],
        out_specs=(hbm, hbm),
        scratch_shapes=[dma((2,))],
        compiler_params=pltpu.CompilerParams(vmem_limit_bytes=1 << 20),
        name="results",
    )(forward, solved)
    return forward.reshape(rhs.shape), solved.reshape(rhs.shape)


def solution(mesh):
    return jax.shard_map(
        on_device,
        mesh=mesh,
        in_specs=(
            P(None, "row", None, None),
            P(None, "col", "row", None, None),
            P(None, "col", "row"),
            P(None, "row", None, None),
        ),
        out_specs=(P(None, "row", None, None), P(None, "row", None, None)),
        check_vma=False,
    )
```

```python
import functools

import jax
import jax.numpy as jnp
from jax import lax
from jax.experimental import pallas as pl
from jax.experimental.pallas import tpu as pltpu
from jax.sharding import PartitionSpec as P

MESH = pl.DeviceIdType.MESH
BF16 = jnp.bfloat16
F32 = jnp.float32


def pair_index(later, earlier):
    return later * (later - 1) // 2 + earlier


def product(left, right, transposed, unit):
    def run(total):
        pltpu.matmul_push_rhs(right, 1, unit, transpose=transposed)
        pltpu.matmul_acc_lhs(total, left, 1)
        return pltpu.matmul_pop(total)

    return pl.run_scoped(run, pltpu.ACC(unit)(left.shape, F32))


def times_transposed(left, right, unit=0):
    return product(left, right, True, unit)


def times(left, right, unit=0):
    return product(left, right, False, unit)


def kernel(
    levels, rows, cols,
    rhs_hbm, factor_hbm, pattern_hbm, diag_hbm, forward_out, solution_out,
    rhs, factor, pattern, diag, dtop, fsend, arecv, zbuf, ebuf, ftop_send, atop, fq, ftop, usend, rrecv, sq, sbuf, pbuf,
    usend0, rrecv0, sbuf0,
    a_send, a_recv, b_send, b_recv, r_send, r_recv, p_send, p_recv, s_send, s_recv, loaded, d_send, d_recv, ready,
):
    row = lax.axis_index("row")
    col = lax.axis_index("col")
    core = col % 2
    chip = col // 2
    home_col = row // 2
    home_chip = home_col // 2
    at_home = chip == home_chip
    own_slot = row % 2
    is_self = at_home & (col == home_col)
    is_server = ((row // 4) % 2 == chip % 2) & ((row // 2) % 2 == core)
    served_row = chip // 2 * 8 + row % 8
    quarter = row // 8
    last = cols // 2 - 1

    def first_of(place):
        return place * (1 - place // last)

    first_chip = first_of(home_chip)
    at_first = chip == first_chip
    is_first_self = at_first & (col == home_col)
    top = levels - 1
    half = fsend.shape[3]
    width = rhs.shape[-1]

    def remote(src, dst, send_sem, recv_sem, device):
        return pltpu.make_async_remote_copy(
            src_ref=src, dst_ref=dst, send_sem=send_sem, recv_sem=recv_sem, device_id=device, device_id_type=MESH
        )

    def send(src, dst, send_sem, recv_sem, device):
        same = (device[0] == row) & (device[1] == col)

        @pl.when(same)
        def _():
            pltpu.make_async_copy(src, dst, recv_sem).start()

        @pl.when(jnp.logical_not(same))
        def _():
            remote(src, dst, send_sem, recv_sem, device).start()

    def await_recv(ref, sem):
        remote(ref, ref, sem, sem, (row, col)).wait_recv()

    def await_sends(count, sem, slots):
        ref = slots.at[0, pl.ds(0, count)]
        remote(ref, ref, sem, sem, (row, col)).wait_send()

    pairs = [(later, earlier) for later in range(1, levels) for earlier in range(later)]
    loads = [
        pltpu.make_async_copy(src, dst, loaded.at[n])
        for n, (src, dst) in enumerate(
            [
                (rhs_hbm, rhs),
                (pattern_hbm, pattern),
                (diag_hbm.at[0], diag.at[0]),
                (factor_hbm.at[pl.ds(0, 2)], factor.at[pl.ds(0, 2)]),
                (diag_hbm.at[pl.ds(1, levels - 1)], diag.at[pl.ds(1, levels - 1)]),
                (factor_hbm.at[pl.ds(2, factor.shape[0] - 2)], factor.at[pl.ds(2, factor.shape[0] - 2)]),
            ]
        )
    ]
    for load in loads:
        load.start()

    barrier = pltpu.get_barrier_semaphore()

    def greet(device):
        same = (device[0] == row) & (device[1] == col)

        @pl.when(jnp.logical_not(same))
        def _():
            pl.semaphore_signal(barrier, inc=1, device_id=device, device_id_type=MESH)

    def ring(step, size):
        return min(step, size - step)

    def nearest_last(steps):
        return sorted(steps, key=lambda s: -ring(s[0], 4) - ring(s[1], 8) - ring(s[2], 8) - s[3] / 2)

    row_steps = nearest_last([(x, y, 0, 0) for x in range(4) for y in range(8)])
    col_steps = nearest_last([(0, 0, z, k) for z in range(cols // 2) for k in range(2)])
    row_by_x = [(quarter + x) % 4 * 8 for x in range(4)]
    row_by_y = [(row + y) % 8 for y in range(8)]
    col_by_z = [(chip + z) % (cols // 2) * 2 for z in range(cols // 2)]
    col_by_core = [core, 1 - core]
    plane = [row_by_x[x] + row_by_y[y] for x, y, _, _ in row_steps]
    column = [col_by_z[z] + col_by_core[k] for _, _, z, k in col_steps]

    first_rows = sorted(range(rows), key=lambda r: ring(r // 8, 4) + ring(r % 8, 8))
    chips = cols // 2

    def repeat(count, step):
        def body(n, _):
            step(n)
            return 0

        lax.fori_loop(0, count, body, 0)

    @pl.when(at_first)
    def _():
        for to_row in plane[:-1]:
            pl.semaphore_signal(barrier, inc=1, device_id=(to_row, home_col), device_id_type=MESH)
        greet((row, home_col))

    for h in range(2):
        greet((row, first_chip * 2 + h))

    def fold(later, earlier):
        index = pair_index(later, earlier)

        for j in range(2):
            block = times(factor[2 * index + j], diag[earlier], j) * pattern[j, 0, index].astype(F32)
            factor[2 * index + j] = block.astype(BF16)

    def joined(ref):
        return ref[...].reshape(2 * half, width)

    def zeta_of(level):
        return rhs[0] if level == 0 else joined(zbuf.at[level])

    def fterm(later, earlier, j):
        return times_transposed(zeta_of(earlier), factor[2 * pair_index(later, earlier) + j], j)

    def bterm(later, earlier, j):
        return times(joined(pbuf.at[later, j]), factor[2 * pair_index(later, earlier) + j], j)

    def prepare(later, earlier, transposed):
        for j in range(2):
            block = factor[2 * pair_index(later, earlier) + j]
            pltpu.matmul_push_rhs(block, 0, j, transpose=transposed)

    def prepared_times(lefts):
        def run(*products):
            for left, total in zip(lefts, products):
                pltpu.matmul_acc_lhs(total, left, 0)
            return [pltpu.matmul_pop(total) for total in products]

        return pl.run_scoped(run, *[pltpu.ACC(j)((2 * half, width), F32) for j in range(2)])

    def finish_forward(level):
        solved = times_transposed(zeta_of(level), diag[level]).astype(BF16)
        forward_out[level] = solved
        ebuf[level] = times(solved, diag[level])

    def await_halves(buf, sem, has_one):
        @pl.when(has_one)
        def _():
            await_recv(buf.at[0], sem)

        @pl.when(jnp.logical_not(has_one))
        def _():
            await_recv(buf, sem)

    def serve(level):
        at = level - 1
        solved, slot = sq.at[level], pbuf.at[level, own_slot, quarter]
        if level > 1:
            for to_row in plane[:-1]:
                remote(solved, slot, p_send.at[at], p_recv.at[at], (to_row, col)).start()
            pltpu.make_async_copy(solved, slot, p_recv.at[at]).start()
        else:
            for to_row in first_rows:
                send(solved, slot, p_send.at[at], p_recv.at[at], (to_row, col))
        give(solved, sbuf.at[level, quarter], s_send.at[level], s_recv.at[level])

    def give(src, dst, send_sem, recv_sem):
        for to_col in column[:-1]:
            remote(src, dst, send_sem, recv_sem, (served_row, to_col)).start()
        send(src, dst, send_sem, recv_sem, (served_row, col))

    for load in loads[:4]:
        load.wait()
    fold(1, 0)
    lower = [fterm(1, 0, j) for j in range(2)]

    for level in range(1, top):
        at = level - 1
        for j in range(2):
            fsend[at, j] = lower[j].astype(BF16).reshape(2, half, width)
        if level == 1:

            @pl.when(jnp.logical_not(at_first))
            def _():
                pl.semaphore_wait(barrier, 4)

            @pl.when(at_first & jnp.logical_not(is_first_self))
            def _():
                pl.semaphore_wait(barrier, 4 + cols - 1)

            @pl.when(is_first_self)
            def _():
                pl.semaphore_wait(barrier, 3 + cols - 1)

        if level == 2:

            @pl.when(chip == last)
            def _():
                pl.semaphore_wait(ready, 4)

        to_chip = first_of(chip) if level == 1 else chip
        for j in range(2):
            for h in range(2):
                to = (2 * col + j, to_chip * 2 + h)
                send(fsend.at[at, j, h], arecv.at[at, row], a_send.at[at], a_recv.at[at], to)

        if level == 1:
            loads[4].wait()
            loads[5].wait()
            for later, earlier in pairs[1:]:
                fold(later, earlier)
        early = [sum(fterm(level + 1, b, j) for b in range(level)) for j in range(2)]
        finish_forward(level - 1)
        prepare(level + 1, level, True)

        @pl.when(at_first if level == 1 else at_home)
        def _():
            await_recv(arecv.at[at], a_recv.at[at])
            total = jnp.sum(arecv[at].astype(F32), axis=0)
            own_half = rhs[level, pl.ds(pl.multiple_of(core * half, half), half)].astype(F32)
            zbuf[level, core] = (own_half - total).astype(BF16)
            own = zbuf.at[level, core]
            for to_col in column[:-1]:
                remote(own, own, b_send.at[at], b_recv.at[at], (row, to_col)).start()
            if level == 1:

                @pl.when(home_chip == last)
                def _():
                    for to_row in plane:
                        pl.semaphore_signal(ready, inc=1, device_id=(to_row, home_col), device_id_type=MESH)

        await_halves(zbuf.at[level], b_recv.at[at], at_first if level == 1 else at_home)
        lower = [early[j] + term for j, term in enumerate(prepared_times([zeta_of(level)] * 2))]
        if level == 1:

            @pl.when(is_self)
            def _():
                for q in range(4):
                    send(diag.at[top], dtop, d_send, d_recv, (q * 8 + row % 8, home_col))

    at = top - 1
    for j in range(2):
        mine = jnp.where(is_self & (own_slot == j), rhs[top].astype(F32) - lower[j], -lower[j])
        ftop_send[j] = mine.astype(BF16).reshape(ftop_send.shape[1:])
    for j in range(2):
        for q in range(4):
            to = (q * 8 + (2 * col + j) % 8, col)
            send(ftop_send.at[j, q], atop.at[row], a_send.at[at], a_recv.at[at], to)
    finish_forward(top - 1)

    @pl.when(is_server)
    def _():
        await_recv(dtop, d_recv)
        await_recv(atop, a_recv.at[at])
        zeta = jnp.sum(atop[...].astype(F32), axis=0).astype(BF16)
        twice = times_transposed(jnp.concatenate([zeta, zeta], axis=0), dtop[...]).astype(BF16)
        fq[...] = twice[: half // 2]
        sq[top] = times(twice, dtop[...])[: half // 2].astype(BF16)
        serve(top)
        give(fq, ftop.at[quarter], b_send.at[at], b_recv.at[at])

    early = None
    for level in range(top - 1, -1, -1):
        prepare(level + 1, level, False)
        await_recv(pbuf.at[level + 1], p_recv.at[level])
        upper = sum(prepared_times([joined(pbuf.at[level + 1, j]) for j in range(2)]))
        if early is not None:
            upper = upper + early
        if level > 0:
            mine = jnp.where(col == home_col, ebuf[level] - upper, -upper)
            usend[level] = mine.astype(BF16).reshape(usend.shape[1:])
            for q in range(4):
                to = (q * 8 + row % 8, home_col)
                send(usend.at[level, q], rrecv.at[level, col], r_send.at[level], r_recv.at[level], to)
            early = sum(bterm(later, level - 1, j) for later in range(level + 1, levels) for j in range(2))

            @pl.when(is_server)
            def _():
                slots = rrecv.at[level, pl.ds(0, cols)]
                await_recv(slots, r_recv.at[level])
                sq[level] = jnp.sum(slots[...].astype(F32), axis=0).astype(BF16)
                serve(level)

    usend0[...] = upper.astype(BF16).reshape(usend0.shape)
    for z in range(chips):
        for k in range(2):
            for h in range(2) if z < 1 else [k]:
                send(usend0.at[h], rrecv0.at[h, col], r_send.at[0], r_recv.at[0], (row, z * 2 + k))
    starts_first = chip < 1

    await_recv(ftop, b_recv.at[top - 1])
    forward_out[top] = joined(ftop)
    for level in range(top, 0, -1):
        await_recv(sbuf.at[level], s_recv.at[level])
        solution_out[level] = joined(sbuf.at[level])

    @pl.when(starts_first)
    def _():
        await_recv(rrecv0, r_recv.at[0])
        total = jnp.sum(rrecv0[...].astype(F32), axis=1).reshape(2 * half, width)
        solution_out[0] = (ebuf[0] - total).astype(BF16)
        await_sends(cols + 2 - 2, r_send.at[0], arecv)

    @pl.when(jnp.logical_not(starts_first))
    def _():
        await_recv(rrecv0.at[core], r_recv.at[0])
        total = jnp.sum(rrecv0[core].astype(F32), axis=0)
        mine = ebuf[0, pl.ds(pl.multiple_of(core * half, half), half)]
        sbuf0[core] = (mine - total).astype(BF16)
        other = (row, chip * 2 + 1 - core)
        remote(sbuf0.at[core], sbuf0.at[core], s_send.at[0], s_recv.at[0], other).start()
        await_recv(sbuf0.at[0], s_recv.at[0])
        solution_out[0] = joined(sbuf0)
        await_sends(1, s_send.at[0], arecv)
        await_sends(cols + 2 - 1, r_send.at[0], arecv)

    def await_all_but(one_less, count, sem, slots):
        pl.when(one_less)(lambda: await_sends(count - 1, sem, slots))
        pl.when(jnp.logical_not(one_less))(lambda: await_sends(count, sem, slots))

    for at in range(top - 1):
        await_all_but(is_first_self if at == 0 else is_self, 4, a_send.at[at], arecv)
    await_all_but(is_server, 8, a_send.at[top - 1], rrecv)
    for level in range(1, top):
        await_all_but(is_self, 4, r_send.at[level], rrecv)

    for at in range(top - 1):
        pl.when(at_first if at == 0 else at_home)(lambda at=at: await_sends(cols - 1, b_send.at[at], arecv))

    @pl.when(is_server)
    def _():
        await_all_but(is_self, cols, b_send.at[top - 1], rrecv)
        for level in range(1, levels):
            await_all_but(is_self, cols, s_send.at[level], rrecv)
            await_sends(rows - 1, p_send.at[level - 1], rrecv)

    @pl.when(is_self)
    def _():
        three = factor.at[pl.ds(0, 3)]
        remote(three, three, d_send, d_send, (row, col)).wait_send()


def copy_out(forward, solved, forward_out, solution_out, sems):
    copies = [
        pltpu.make_async_copy(forward, forward_out, sems.at[0]),
        pltpu.make_async_copy(solved, solution_out, sems.at[1]),
    ]
    for copy in copies:
        copy.start()
    for copy in copies:
        copy.wait()


def on_device(rhs, factor, pattern, diag_inverse):
    levels, _, count, width = rhs.shape
    pairs, block_rows = factor.shape[:2]
    rows, cols = lax.axis_size("row"), lax.axis_size("col")
    half = count // 2
    steps = levels - 1
    vmem, hbm = pl.BlockSpec(memory_space=pltpu.VMEM), pl.BlockSpec(memory_space=pltpu.HBM)
    dma = pltpu.SemaphoreType.DMA
    out = pltpu.VMEM((levels, count, width), BF16)
    forward, solved = pl.pallas_call(
        functools.partial(kernel, levels, rows, cols),
        out_shape=(out, out),
        in_specs=[hbm, hbm, hbm, hbm],
        out_specs=(vmem, vmem),
        scratch_shapes=[
            pltpu.VMEM((levels, count, width), BF16),
            pltpu.VMEM((pairs * block_rows, width, width), BF16),
            pltpu.SMEM((block_rows, 1, pairs), jnp.int32),
            pltpu.VMEM((levels, width, width), BF16),
            pltpu.VMEM((width, width), BF16),
            pltpu.VMEM((steps - 1, 2, 2, half, width), BF16),
            pltpu.VMEM((steps - 1, rows, half, width), BF16),
            pltpu.VMEM((steps, 2, half, width), BF16),
            pltpu.VMEM((steps, count, width), F32),
            pltpu.VMEM((2, 4, half // 2, width), BF16),
            pltpu.VMEM((rows, half // 2, width), BF16),
            pltpu.VMEM((half // 2, width), BF16),
            pltpu.VMEM((4, half // 2, width), BF16),
            pltpu.VMEM((steps, 4, half // 2, width), BF16),
            pltpu.VMEM((steps, rows, half // 2, width), BF16),
            pltpu.VMEM((levels, half // 2, width), BF16),
            pltpu.VMEM((levels, 4, half // 2, width), BF16),
            pltpu.VMEM((levels, 2, 4, half // 2, width), BF16),
            pltpu.VMEM((2, half, width), BF16),
            pltpu.VMEM((2, cols, half, width), BF16),
            pltpu.VMEM((2, half, width), BF16),
        ]
        + [dma((steps,))] * 8
        + [dma((levels,))] * 2
        + [dma((6,))]
        + [dma, dma, pltpu.SemaphoreType.REGULAR],
        compiler_params=pltpu.CompilerParams(collective_id=0, has_side_effects=True),
        name="solves",
    )(
        rhs.reshape(levels, count, width),
        factor.reshape(pairs * block_rows, width, width),
        pattern.transpose(1, 2, 0),
        diag_inverse.reshape(levels, width, width),
    )
    out = jax.ShapeDtypeStruct((levels, count, width), BF16)
    forward, solved = pl.pallas_call(
        copy_out,
        out_shape=(out, out),
        in_specs=[vmem, vmem],
        out_specs=(hbm, hbm),
        scratch_shapes=[dma((2,))],
        compiler_params=pltpu.CompilerParams(vmem_limit_bytes=1 << 20),
        name="results",
    )(forward, solved)
    return forward.reshape(rhs.shape), solved.reshape(rhs.shape)


def solution(mesh):
    return jax.shard_map(
        on_device,
        mesh=mesh,
        in_specs=(
            P(None, "row", None, None),
            P(None, "col", "row", None, None),
            P(None, "col", "row"),
            P(None, "row", None, None),
        ),
        out_specs=(P(None, "row", None, None), P(None, "row", None, None)),
        check_vma=False,
    )
```
